256 devices in a mesh: bulk: 64 (over z, x, core), slab: 4 (over y).
Axes of the slice: x: 4, y: 4, z: 8, core: 2. Of those that a mesh axis runs over, the one named last changes fastest.
Arguments:
- pressure: float32 [1024, 256, 128], P('bulk', 'slab'), may hold values from -12 to 12
- rhs: float32 [1024, 256, 128], P('bulk', 'slab'), may hold values from -48 to 48
- kappa: float32 [1024, 256, 128], P('bulk', 'slab'), may hold values from 0.5 to 8
- owner: int32 [4, 64, 1024, 1], P('slab', 'bulk'), may hold values from 0 to 63; in each aligned block of 1024 rows (0 to 1023, 1024 to 2047, ..., all dimensions but the last counted through in order) at most 40 rows name the same one
- coarse_row: int32 [4, 64, 1024], P('slab', 'bulk'), may hold values from 0 to 127
- coarse_leak: float32 [4, 8192, 128], P('slab', 'bulk'), may hold values from 1 to 16
- coarse_link: float32 [4, 8192, 128], P('slab', 'bulk'), may hold values from 1 to 16
Outputs:
- pressure_out: float32 [1024, 256, 128], P('bulk', 'slab')
The draws below stay inside these ranges and needn't reach their ends.
Inputs may be any that keep to these rules, and one draw needn't show every extreme that they name: Among the 1024 fine rows of one device, at most 40 name the same owner; in every draw some device gives exactly 40 rows to some owner.
All inputs are finite; a program needn't handle non-finite values.
Results may differ from the reference program's by a relative error of at most 0.00002.
Values sent between devices are 32-bit elements; how exact they have to be, the bound alone decides.
No kernel may reach another device: no remote copies, remote signals or barrier semaphores. Data moves between devices by JAX's collectives and lax.ppermute only.
A program may use at most 64 MiB of HBM per device.

```python
import math
import jax
import jax.numpy as jnp
import numpy as np

CX = 16
CY = 64
NZ = 128
SWEEPS = 2
COARSE_SWEEPS = 3
CR = 128
CAP = 40
NX = 1024
NY = 256
N_BULK = 64
N_SLAB = 4


def set_ends(entries, stream_key, smallest, top_value):
    index_at = [jax.random.randint(jax.random.fold_in(stream_key, axis), (), 0, length) for axis, length in enumerate(entries.shape)]
    widest = entries.shape.index(max(entries.shape))
    next_to = index_at[:widest] + [(index_at[widest] + 1) % entries.shape[widest]] + index_at[widest + 1:]
    return entries.at[tuple(index_at)].set(smallest).at[tuple(next_to)].set(top_value)


def shard_levels(key, extent, cuts, smallest, high):
    factor_of, own = 1.0, jax.random.fold_in(key, 6)
    for position, shards_of in cuts:
        heights = jnp.exp(jax.random.uniform(jax.random.fold_in(own, position), (shards_of,), jnp.float32, smallest / len(cuts), high / len(cuts)))
        factor_of = factor_of * jnp.repeat(heights, extent[position] // shards_of).reshape([-1 if axis == position else 1 for axis in range(len(extent))])
    return factor_of


def deal_out(key, own, number, rows, amount, top, most, lean):
    ranking = jax.random.permutation(key, amount)
    heavy_load, ordinary = portions_of(amount, rows * top, most, lean, True), portions_of(amount, rows * top, most, lean, False)
    places = jnp.arange(amount)

    def named(tallies, turn):
        used = int((tallies > 0).sum())
        fixed = max(1, used // 4)
        shifted = fixed + (places - fixed + turn * (used - fixed)) % max(1, amount - fixed)
        return jnp.zeros((amount,), jnp.int32).at[ranking[jnp.where(places < fixed, places, shifted)]].set(jnp.asarray(tallies, jnp.int32))

    tallies = jnp.where(number % 4 == 0, named(heavy_load, number // 4), named(ordinary, number - number // 4 - 1))
    mixed = jax.random.permutation(jax.random.fold_in(own, 3), amount)
    donor, sink = mixed[0:amount // 2 * 2:2], mixed[1:amount // 2 * 2:2]
    margin = jnp.minimum(tallies[donor] - 1, most - tallies[sink]) // 2
    margin = jnp.where((donor == ranking[0]) | (sink == ranking[0]) | (tallies[sink] == 0), 0, jnp.maximum(margin, 0))
    shifted = jax.random.randint(jax.random.fold_in(own, 4), (amount // 2,), 0, 1 << 20) % (margin + 1)
    tallies = tallies.at[donor].add(-shifted).at[sink].add(shifted)
    labels = jnp.searchsorted(jnp.cumsum(tallies), jnp.arange(rows * top), side="right").astype(jnp.int32)
    table = labels.reshape(top, rows).T
    table = table[jax.random.permutation(jax.random.fold_in(own, 1), rows)]
    turn = jax.random.randint(jax.random.fold_in(own, 2), (rows, 1), 0, top)
    return jnp.take_along_axis(table, (jnp.arange(top)[None, :] + turn) % top, axis=1)


def portions_of(amount, total, limit, skew, full):
    loads = [(1 << 20) // math.isqrt(rank ** skew) + 1 for rank in range(1, amount + 1)]
    largest = limit if full else min(limit, max(-(-total // amount), total * loads[0] // sum(loads)))
    least = 1 if total - largest >= amount - 1 else 0
    given, surplus = [largest] + [least] * (amount - 1), total - largest - least * (amount - 1)
    while surplus > 0:
        movable = [i for i in range(1, amount) if given[i] < largest] or [i for i in range(1, amount) if given[i] < limit]
        whole, remaining = sum([loads[i] for i in movable]), surplus
        for i in movable:
            more = min(limit - given[i], max(1, remaining * loads[i] // whole), surplus)
            given[i] = given[i] + more
            surplus = surplus - more
    return np.array(given)


def bell_draw(rng, extent, spread, limit, pieces=(), held_as=jnp.bfloat16):
    gain = shard_levels(rng, extent, pieces, -0.22, 0.18) if pieces else 1.0
    values = jax.random.normal(rng, extent, jnp.float32) * spread * gain
    return jnp.minimum(jnp.maximum(values, -limit), limit).astype(held_as)


def setup_inputs(seed: int = 0) -> dict:
    key_of = jax.random.split(jax.random.key(seed), 8)
    pressure = bell_draw(key_of[0], (NX, NY, NZ), 2.0, 12.0, ((0, 64), (1, 4)), jnp.float32)
    rhs = bell_draw(key_of[1], (NX, NY, NZ), 8.0, 48.0, ((0, 64), (1, 4)), jnp.float32)
    kappa = jnp.clip(jnp.exp(math.log(8.0) - 2.7725887 * jax.random.uniform(key_of[2], (NX, NY, NZ), jnp.float32) ** shard_levels(key_of[2], (NX, NY, NZ), ((0, 64), (1, 4)), -0.2, 0.2)), 0.5, 8.0)
    owner_keys = jax.random.split(jax.random.fold_in(key_of[3], 1), N_SLAB * N_BULK * (CX * CY) // (CX * CY))
    owner_turns = jax.random.permutation(jax.random.fold_in(key_of[3], 3), N_SLAB * N_BULK * (CX * CY) // (CX * CY))
    owner = jax.vmap(lambda own, number: deal_out(jax.random.fold_in(key_of[3], 2), own, number, CX * CY, N_BULK, 1, CAP, 1))(owner_keys, owner_turns).reshape((N_SLAB, N_BULK, CX * CY, 1))
    coarse_row = set_ends(jax.random.randint(key_of[4], (N_SLAB, N_BULK, CX * CY), 0, CR), jax.random.fold_in(key_of[4], 1), 0, CR - 1).astype(jnp.int32)
    coarse_leak = jnp.clip(jnp.exp(math.log(16.0) - 2.7725887 * jax.random.uniform(key_of[5], (N_SLAB, N_BULK * CR, NZ), jnp.float32) ** shard_levels(key_of[5], (N_SLAB, N_BULK * CR, NZ), ((0, 4), (1, 64)), -0.2, 0.2)), 1.0, 16.0)
    coarse_link = jnp.clip(jnp.exp(math.log(16.0) - 2.7725887 * jax.random.uniform(key_of[6], (N_SLAB, N_BULK * CR, NZ), jnp.float32) ** shard_levels(key_of[6], (N_SLAB, N_BULK * CR, NZ), ((0, 4), (1, 64)), -0.2, 0.2)), 1.0, 16.0)
    return dict(pressure=pressure, rhs=rhs, kappa=kappa, owner=owner, coarse_row=coarse_row, coarse_leak=coarse_leak, coarse_link=coarse_link)


damping = 0.8


def shift_up(values):
    return jnp.concatenate([values[..., 1:], jnp.zeros_like(values[..., :1])], axis=-1)


def shift_down(values):
    return jnp.concatenate([jnp.zeros_like(values[..., :1]), values[..., :-1]], axis=-1)


def pad_plane(values):
    return jnp.pad(values, ((1, 1), (1, 1), (0, 0)))


def face_set(kappa, kappa_rims):
    west_face = 0.5 * (kappa + kappa_rims[:-2, 1:-1])
    east_face = 0.5 * (kappa + kappa_rims[2:, 1:-1])
    south_face = 0.5 * (kappa + kappa_rims[1:-1, :-2])
    north_face = 0.5 * (kappa + kappa_rims[1:-1, 2:])
    lower_face = 0.5 * (kappa + shift_down(kappa))
    upper_face = 0.5 * (kappa + shift_up(kappa))
    faces = (west_face, east_face, south_face, north_face, lower_face, upper_face)
    diagonal = west_face + east_face + south_face + north_face + lower_face + upper_face
    return faces, diagonal


def operate(field, field_rims, faces):
    west_face, east_face, south_face, north_face, lower_face, upper_face = faces
    result = west_face * (field - field_rims[:-2, 1:-1]) + east_face * (field - field_rims[2:, 1:-1])
    result = result + south_face * (field - field_rims[1:-1, :-2]) + north_face * (field - field_rims[1:-1, 2:])
    result = result + lower_face * (field - shift_down(field)) + upper_face * (field - shift_up(field))
    return result


def coarse_smooth(coarse_rhs, leak, link):
    link_below = shift_down(link)
    cdiag = leak + link + link_below
    correction = jnp.zeros_like(coarse_rhs)
    for sweep_index in range(COARSE_SWEEPS):
        applied = leak * correction + link * (correction - shift_up(correction)) + link_below * (correction - shift_down(correction))
        correction = correction + damping * (coarse_rhs - applied) / cdiag
    return correction


def reference(pressure, rhs, kappa, owner, coarse_row, coarse_leak, coarse_link):
    faces, diagonal = face_set(kappa, pad_plane(kappa))
    field = pressure
    for sweep_index in range(SWEEPS):
        field = field + damping * (rhs - operate(field, pad_plane(field), faces)) / diagonal
    residual = rhs - operate(field, pad_plane(field), faces)
    residual_rows = residual.reshape(N_BULK, CX, N_SLAB, CY, NZ).transpose(2, 0, 1, 3, 4).reshape(N_SLAB * N_BULK * CX * CY, NZ)
    coarse_index = owner.reshape(N_SLAB, N_BULK * CX * CY).astype(jnp.int32) * CR + coarse_row.reshape(N_SLAB, N_BULK * CX * CY).astype(jnp.int32)
    flat_index = (coarse_index + (jnp.arange(N_SLAB, dtype=jnp.int32) * (N_BULK * CR))[:, None]).reshape(-1)
    coarse_rhs = jax.ops.segment_sum(residual_rows, flat_index, num_segments=N_SLAB * N_BULK * CR)
    leak = coarse_leak.reshape(N_SLAB * N_BULK * CR, NZ)
    link = coarse_link.reshape(N_SLAB * N_BULK * CR, NZ)
    correction = coarse_smooth(coarse_rhs, leak, link)
    fine_correction = correction[flat_index].reshape(N_SLAB, N_BULK, CX, CY, NZ).transpose(1, 2, 0, 3, 4).reshape(NX, NY, NZ)
    field = field + fine_correction
    for sweep_index in range(SWEEPS):
        field = field + damping * (rhs - operate(field, pad_plane(field), faces)) / diagonal
    return field
```

```python
import jax
import jax.numpy as jnp
from jax import lax
from jax.experimental import pallas as pl
from jax.experimental.pallas import tpu as pltpu
from jax.sharding import PartitionSpec as P

DAMPING = 0.8
CX, CY, NZ = 16, 64, 128
CR = 128
CAP = 40
BLOCK = CAP + 1
TRIO = 3 * BLOCK
W = 3
TOP = 8
EX, EY = CX + 2 * W, CY + 2 * TOP
F32, BF16, I32 = jnp.float32, jnp.bfloat16, jnp.int32

VMEM = pl.BlockSpec(memory_space=pltpu.VMEM)
SMEM = pl.BlockSpec(memory_space=pltpu.SMEM)


def iota(shape, dim):
    return lax.broadcasted_iota(I32, shape, dim)


def call(kernel, outs, args, in_specs=None, scratch=(), mib=16, aliases=None, out_specs=None):
    return pl.pallas_call(
        kernel,
        out_shape=[jax.ShapeDtypeStruct(s, d) for s, d in outs],
        in_specs=in_specs or [VMEM] * len(args),
        out_specs=out_specs or [VMEM] * len(outs),
        scratch_shapes=list(scratch),
        input_output_aliases=aliases or {},
        compiler_params=pltpu.CompilerParams(vmem_limit_bytes=mib << 20),
    )(*args)


def slot_kernel(owners, own_ref, row_ref, slot_ref, buf_ref):
    shift = lax.rem(lax.axis_index("bulk"), 3) * BLOCK
    before = (iota((128, 128), 0) < iota((128, 128), 1)).astype(BF16)
    owner_of = iota((owners, 128), 0)
    lane_of = iota((128, 128), 0)
    seen = jnp.zeros((owners, 1), F32)
    numbers = jnp.zeros((owners, 128), F32)
    for b in range(own_ref.shape[0]):
        own = own_ref[b : b + 1, :]
        mine = owner_of == own
        mine_f = mine.astype(F32)
        count = jnp.dot(mine_f.astype(BF16), before, preferred_element_type=F32) + seen
        rank = jnp.sum(jnp.where(mine, count, 0.0), axis=0, keepdims=True).astype(I32)
        seen = seen + jnp.sum(mine_f, axis=1, keepdims=True)
        slot_ref[b : b + 1, :] = own * BLOCK + rank
        named = jnp.where(lane_of == rank + shift, (row_ref[b : b + 1, :] + 1).astype(F32), 0.0)
        numbers = numbers + lax.dot_general(
            mine_f.astype(BF16), named.astype(BF16), (((1,), (1,)), ((), ())), preferred_element_type=F32
        )
    buf_ref[...] = jnp.zeros_like(buf_ref)
    for o in range(owners):
        buf_ref[o * BLOCK + CAP : o * BLOCK + BLOCK, :] = numbers[o : o + 1, :]


def inside_rows(low, high):
    y = iota((EY, NZ), 0)
    return ((y >= TOP) | low) & ((y < TOP + CY) | high)


def edges():
    b, s = lax.axis_index("bulk"), lax.axis_index("slab")
    return b > 0, b < lax.axis_size("bulk") - 1, s > 0, s < lax.axis_size("slab") - 1


def prepare(k_ref, wx, wy, wz, q, first, last):
    xl, xh, yl, yh = edges()
    z = iota((EY, NZ), 1)
    rows_in = inside_rows(yl, yh)

    def body(x, carry):
        k = k_ref[x]
        wxl, wxh = k + k_ref[x - 1], k + k_ref[x + 1]
        wyl, wyh = k + pltpu.roll(k, 1, 0), k + pltpu.roll(k, EY - 1, 0)
        ks = jnp.where(z == 0, 0.0, pltpu.roll(k, 1, 1))
        kn = jnp.where(z == NZ - 1, 0.0, pltpu.roll(k, NZ - 1, 1))
        diagonal = (wxl + wxh) + (wyl + wyh) + ((k + ks) + (k + kn))
        ok = rows_in & ((x >= W) | xl) & ((x < W + CX) | xh) & (diagonal > 0.0)
        q[x] = jnp.where(ok, DAMPING / jnp.where(ok, diagonal, 1.0), 0.0)
        wx[x] = wxl
        wy[x] = wyl
        wz[x] = jnp.where(z == 0, 0.0, k + ks)
        return carry

    lax.fori_loop(first, last, body, 0)
    wx[last] = k_ref[last] + k_ref[last - 1]


def neighbours(x, v_ref, wx, wy, wz):
    v = v_ref[x]
    wyl, wzl = wy[x], wz[x]
    total = wx[x] * v_ref[x - 1] + wx[x + 1] * v_ref[x + 1]
    total = total + wyl * pltpu.roll(v, 1, 0) + pltpu.roll(wyl * v, EY - 1, 0)
    total = total + wzl * pltpu.roll(v, 1, 1) + pltpu.roll(wzl * v, NZ - 1, 1)
    return v, total


def sweep(old, new, r2, wx, wy, wz, q, first, last):
    def body(x, carry):
        v, total = neighbours(x, old, wx, wy, wz)
        new[x] = (1.0 - DAMPING) * v + q[x] * (r2[x] + total)
        return carry

    lax.fori_loop(first, last, body, 0)


def pre_kernel(
    slot, p_ref, r_ref, k_ref, bl, bh, sl, sh, buf_in, vout, buf, kx, rx, va, vb, wx, wy, wz, q, res
):
    del buf_in
    xl, xh, yl, yh = edges()
    zero = jnp.zeros((EY, NZ), F32)

    def fill(dst, own, a, scale):
        for x in range(EX):
            dst[x, 0:TOP, :] = zero[0:TOP]
            dst[x, TOP + CY :, :] = zero[0:TOP]
            if x < W:
                mid, ok = bl[a * W + x], xl
            elif x < W + CX:
                mid, ok = own[x - W], None
            else:
                mid, ok = bh[a * W + x - W - CX], xh
            lo, hi = sl[a * EX + x], sh[a * EX + x]
            oky, okz = (yl, yh) if ok is None else (yl & ok, yh & ok)
            if ok is not None:
                mid = jnp.where(ok, mid, 0.0)
            dst[x, TOP : TOP + CY, :] = mid * scale if scale != 1 else mid
            dst[x, TOP - W : TOP, :] = jnp.where(oky, lo, 0.0) * scale
            dst[x, TOP + CY : TOP + CY + W, :] = jnp.where(okz, hi, 0.0) * scale

    fill(va, p_ref, 0, 1.0)
    fill(rx, r_ref, 1, 2.0)
    fill(kx, k_ref, 2, 1.0)
    prepare(kx, wx, wy, wz, q, 1, EX - 1)
    sweep(va, vb, rx, wx, wy, wz, q, 1, EX - 1)
    sweep(vb, va, rx, wx, wy, wz, q, 2, EX - 2)
    for x in range(CX):
        vout[x] = va[x + W, TOP : TOP + CY, :]

    def residual(x, carry):
        v, total = neighbours(x + W, va, wx, wy, wz)
        d = DAMPING / jnp.where(q[x + W] == 0.0, 1.0, q[x + W])
        out = 0.5 * ((rx[x + W] + total) - d * v)
        res[pl.ds(pl.multiple_of(x * CY, CY), CY), :] = out[TOP : TOP + CY]
        return carry

    lax.fori_loop(0, CX, residual, 0)

    def put(i, carry):
        for u in range(16):
            r = i * 16 + u
            buf[pl.ds(slot[r], 1), :] = res[pl.ds(r, 1), :]
        return carry

    lax.fori_loop(0, CX * CY // 16, put, 0)


def parts_of(x):
    a = x.astype(BF16)
    rest = x - a.astype(F32)
    b = rest.astype(BF16)
    return a, b, (rest - b.astype(F32)).astype(BF16)


def coarse_kernel(owners, data, leak_ref, link_ref, back, hot):
    rows = owners * BLOCK
    groups = -(-owners // 3)
    number = (iota((CR, 128), 0) + 1).astype(F32)
    total = jnp.zeros((CR, NZ), F32)
    bases = []
    for g in range(groups):
        base = g * TRIO
        names = [data[base + t * BLOCK + CAP : base + (t + 1) * BLOCK, :] for t in range(min(3, owners - 3 * g))]
        name = names[0]
        for more in names[1:]:
            name = name + more
        if base + 128 > rows:
            name = pltpu.roll(jnp.broadcast_to(name, (8, 128)), base - (rows - 128), 1)[0:1]
            base = rows - 128
        bases.append(base)
        one_hot = jnp.where(number == name, 1.0, 0.0).astype(BF16)
        hot[g] = one_hot
        for part in parts_of(data[base : base + 128, :]):
            total = total + jnp.dot(one_hot, part, preferred_element_type=F32)

    z = iota((CR, NZ), 1)
    link = link_ref[...]
    inner = jnp.where(z == NZ - 1, 0.0, link)
    below = pltpu.roll(inner, 1, 1)
    w = DAMPING / (leak_ref[...] + link + below)
    u = w * total
    for _ in range(2):
        u = (1.0 - DAMPING) * u + w * (total + inner * pltpu.roll(u, NZ - 1, 1) + pltpu.roll(inner * u, 1, 1))
    pieces = parts_of(u)
    for g in range(groups - 1, -1, -1):
        out = jnp.zeros((128, NZ), F32)
        for part in pieces:
            out = out + lax.dot_general(hot[g], part, (((0,), (0,)), ((), ())), preferred_element_type=F32)
        if g == groups - 1:
            back[bases[g] : bases[g] + 128, :] = out
        else:
            back[bases[g] : bases[g] + TRIO, :] = out[0:TRIO]


def correct_kernel(slot, back, v_ref, out):
    def take(i, carry):
        for u in range(16):
            r = i * 16 + u
            out[pl.ds(r, 1), :] = back[pl.ds(slot[r], 1), :]
        return carry

    lax.fori_loop(0, CX * CY // 16, take, 0)
    out[...] = out[...] + v_ref[...]


def post_kernel(v_ref, bl, bh, sl, sh, kx, rx, out, va, vb, wx, wy, wz, q):
    xl, xh, yl, yh = edges()
    zero = jnp.zeros((EY, NZ), F32)
    for e in range(1, EX - 1):
        va[e] = zero
        if e < W:
            mid, ok = bl[e - 1], xl
        elif e < W + CX:
            mid, ok = v_ref[e - W], None
        else:
            mid, ok = bh[e - W - CX], xh
        va[e, TOP : TOP + CY, :] = mid if ok is None else jnp.where(ok, mid, 0.0)
        if 2 <= e < EX - 2:
            oky, okz = (yl, yh) if ok is None else (yl & ok, yh & ok)
            va[e, TOP - 2 : TOP, :] = jnp.where(oky, sl[e - 2], 0.0)
            va[e, TOP + CY : TOP + CY + 2, :] = jnp.where(okz, sh[e - 2], 0.0)
    prepare(kx, wx, wy, wz, q, 2, EX - 2)
    sweep(va, vb, rx, wx, wy, wz, q, 2, EX - 2)

    def body(x, carry):
        v, total = neighbours(x + W, vb, wx, wy, wz)
        new = (1.0 - DAMPING) * v + q[x + W] * (rx[x + W] + total)
        out[x] = new[TOP : TOP + CY]
        return carry

    lax.fori_loop(0, CX, body, 0)


def ring(axis, step):
    n = lax.axis_size(axis)
    return [(i, (i + step) % n) for i in range(n)]


def from_both(axis, to_high, to_low):
    return lax.ppermute(to_high, axis, ring(axis, 1)), lax.ppermute(to_low, axis, ring(axis, -1))


def per_device(pressure, rhs, kappa, owner, coarse_row, coarse_leak, coarse_link):
    owners = lax.axis_size("bulk")
    slots = owners * BLOCK
    fields = (pressure, rhs, kappa)
    bl, bh = from_both(
        "bulk",
        jnp.concatenate([f[CX - W :] for f in fields], axis=0),
        jnp.concatenate([f[:W] for f in fields], axis=0),
    )

    def side(lo, hi):
        return jnp.concatenate(
            [
                t
                for a, f in enumerate(fields)
                for t in (bl[a * W : a * W + W, lo:hi], f[:, lo:hi], bh[a * W : a * W + W, lo:hi])
            ],
            axis=0,
        )

    sl, sh = from_both("slab", side(CY - W, CY), side(0, W))
    slot, buf = call(
        lambda *refs: slot_kernel(owners, *refs),
        [((8, 128), I32), ((slots, NZ), F32)],
        (owner.reshape(8, 128), coarse_row.reshape(8, 128)),
    )
    slot = slot.reshape(CX * CY)
    ext = pltpu.VMEM((EX, EY, NZ), F32)
    v, buf, kx, rx = call(
        pre_kernel,
        [((CX, CY, NZ), F32), ((slots, NZ), F32), ((EX, EY, NZ), F32), ((EX, EY, NZ), F32)],
        (slot, pressure, rhs, kappa, bl, bh, sl, sh, buf),
        in_specs=[SMEM] + [VMEM] * 8,
        scratch=[ext] * 6 + [pltpu.VMEM((CX * CY, NZ), F32)],
        aliases={8: 1},
        mib=24,
    )
    sent = lax.all_to_all(buf.reshape(owners, BLOCK, 1, NZ), "bulk", 0, 0)
    (back,) = call(
        lambda *refs: coarse_kernel(owners, *refs),
        [((slots, NZ), F32)],
        (sent.reshape(slots, NZ), coarse_leak[0], coarse_link[0]),
        scratch=[pltpu.VMEM((-(-owners // 3), CR, 128), BF16)],
    )
    got = lax.all_to_all(back.reshape(owners, BLOCK, 1, NZ), "bulk", 0, 0)
    (v,) = call(
        correct_kernel,
        [((CX * CY, NZ), F32)],
        (slot, got.reshape(slots, NZ), v.reshape(CX * CY, NZ)),
        in_specs=[SMEM, VMEM, VMEM],
    )
    v = v.reshape(CX, CY, NZ)
    bl, bh = from_both("bulk", v[CX - 2 :], v[:2])

    def rim(lo, hi):
        return jnp.concatenate([bl[1:, lo:hi], v[:, lo:hi], bh[:1, lo:hi]], axis=0)

    sl, sh = from_both("slab", rim(CY - 2, CY), rim(0, 2))
    (out,) = call(
        post_kernel,
        [((CX, CY, NZ), F32)],
        (v, bl, bh, sl, sh, kx, rx),
        scratch=[ext] * 6,
        mib=24,
    )
    return out


def solution(mesh):
    return jax.shard_map(
        per_device,
        mesh=mesh,
        in_specs=(
            P("bulk", "slab", None),
            P("bulk", "slab", None),
            P("bulk", "slab", None),
            P("slab", "bulk", None, None),
            P("slab", "bulk", None),
            P("slab", "bulk", None),
            P("slab", "bulk", None),
        ),
        out_specs=P("bulk", "slab", None),
        check_vma=False,
    )
```

```python
import jax
import jax.numpy as jnp
from jax import lax
from jax.experimental import pallas as pl
from jax.experimental.pallas import tpu as pltpu
from jax.sharding import PartitionSpec as P

DAMPING = 0.8
CX, CY, NZ = 16, 64, 128
CR = 128
CAP = 40
BLOCK = CAP + 1
TRIO = 3 * BLOCK
W = 3
TOP = 8
EX, EY = CX + 2 * W, CY + 2 * TOP
F32, BF16, I32 = jnp.float32, jnp.bfloat16, jnp.int32

VMEM = pl.BlockSpec(memory_space=pltpu.VMEM)
SMEM = pl.BlockSpec(memory_space=pltpu.SMEM)


def iota(shape, dim):
    return lax.broadcasted_iota(I32, shape, dim)


def call(kernel, outs, args, in_specs=None, scratch=(), mib=16, aliases=None, out_specs=None):
    return pl.pallas_call(
        kernel,
        out_shape=[jax.ShapeDtypeStruct(s, d) for s, d in outs],
        in_specs=in_specs or [VMEM] * len(args),
        out_specs=out_specs or [VMEM] * len(outs),
        scratch_shapes=list(scratch),
        input_output_aliases=aliases or {},
        compiler_params=pltpu.CompilerParams(vmem_limit_bytes=mib << 20),
    )(*args)


def slot_kernel(owners, own_ref, row_ref, slot_ref, buf_ref):
    shift = lax.rem(lax.axis_index("bulk"), 3) * BLOCK
    before = (iota((128, 128), 0) < iota((128, 128), 1)).astype(BF16)
    owner_of = iota((owners, 128), 0)
    lane_of = iota((128, 128), 0)
    seen = jnp.zeros((owners, 1), F32)
    numbers = jnp.zeros((owners, 128), F32)
    for b in range(own_ref.shape[0]):
        own = own_ref[b : b + 1, :]
        mine = owner_of == own
        mine_f = mine.astype(F32)
        count = jnp.dot(mine_f.astype(BF16), before, preferred_element_type=F32) + seen
        rank = jnp.sum(jnp.where(mine, count, 0.0), axis=0, keepdims=True).astype(I32)
        seen = seen + jnp.sum(mine_f, axis=1, keepdims=True)
        slot_ref[b : b + 1, :] = own * BLOCK + rank
        named = jnp.where(lane_of == rank + shift, (row_ref[b : b + 1, :] + 1).astype(F32), 0.0)
        numbers = numbers + lax.dot_general(
            mine_f.astype(BF16), named.astype(BF16), (((1,), (1,)), ((), ())), preferred_element_type=F32
        )
    buf_ref[...] = jnp.zeros_like(buf_ref)
    for o in range(owners):
        buf_ref[o * BLOCK + CAP : o * BLOCK + BLOCK, :] = numbers[o : o + 1, :]


def edges():
    b, s = lax.axis_index("bulk"), lax.axis_index("slab")
    return b > 0, b < lax.axis_size("bulk") - 1, s > 0, s < lax.axis_size("slab") - 1


def zero_index():
    return jnp.minimum(lax.axis_index("bulk"), 0)


def keep(ok, values):
    return values if ok is None else jnp.where(ok, values, 0.0)


def plane_ok(e, xl, xh):
    return xl if e < W else (None if e < W + CX else xh)


def send_kernel(p_ref, k_ref, r_ref, to_high, to_low):
    at = 0
    for ref, n in ((p_ref, W), (k_ref, W), (r_ref, W - 1)):
        to_high[at : at + n] = ref[CX - n : CX]
        to_low[at : at + n] = ref[0:n]
        at += n


def halo_plane(refs, a, e):
    own, bl, bh = refs[a], refs[3], refs[4]
    if W <= e < W + CX:
        return own, e - W
    at = W * a
    if e < W:
        return bl, at + e - (1 if a == 2 else 0)
    return bh, at + e - W - CX


def side_kernel(p_ref, k_ref, r_ref, bl, bh, slot, to_high, to_low):
    del slot
    refs = (p_ref, k_ref, r_ref, bl, bh)
    for e in range(1, EX - 1):
        at = 0
        for a, n in ((0, W), (1, W), (2, W - 1)):
            ref, i = halo_plane(refs, a, e)
            to_high[e - 1, at : at + n, :] = ref[i, CY - n : CY, :]
            to_low[e - 1, at : at + n, :] = ref[i, 0:n, :]
            at += n


def prepare_rows(x, k_ref, wx, wy, wz, q, start, n, wy_start, ok, z):
    rows = pl.ds(start, n)
    k = k_ref[x, rows, :]
    low, high = k_ref[x, pl.ds(start - 1, n), :], k_ref[x, pl.ds(start + 1, n), :]
    wxl = k + k_ref[x - 1, rows, :]
    ks = jnp.where(z == 0, 0.0, pltpu.roll(k, 1, 1))
    kn = jnp.where(z == NZ - 1, 0.0, pltpu.roll(k, NZ - 1, 1))
    wzl = k + ks
    diagonal = (wxl + (k + k_ref[x + 1, rows, :])) + ((k + low) + (k + high)) + (wzl + (k + kn))
    ok = ok & (diagonal > 0.0)
    q[x, rows, :] = jnp.where(ok, DAMPING / jnp.where(ok, diagonal, 1.0), 0.0)
    wx[x, rows, :] = wxl
    wz[x, rows, :] = jnp.where(z == 0, 0.0, wzl)
    if wy_start is None:
        wy[x, rows, :] = k + low
    else:
        wy[x, pl.ds(wy_start, n), :] = k_ref[x, pl.ds(wy_start, n), :] + k_ref[x, pl.ds(wy_start - 1, n), :]


def neighbours(x, v_ref, wx, wy, wz, start, n, off):
    rows, below, above = pl.ds(start, n), pl.ds(off + (start - 1), n), pl.ds(off + (start + 1), n)
    v = v_ref[x, rows, :]
    wzl = wz[x, rows, :]
    total = wx[x, rows, :] * v_ref[x - 1, rows, :] + wx[x + 1, rows, :] * v_ref[x + 1, rows, :]
    total = total + (wy[x, rows, :] * v_ref[x, below, :] + wy[x, above, :] * v_ref[x, above, :])
    return v, total + (wzl * pltpu.roll(v, 1, 1) + pltpu.roll(wzl * v, NZ - 1, 1))


def sweep_rows(x, old, r2, wx, wy, wz, q, start, n, off):
    v, total = neighbours(x, old, wx, wy, wz, start, n, off)
    rows = pl.ds(start, n)
    return (1.0 - DAMPING) * v + q[x, rows, :] * (r2[x, rows, :] + total)


def residual_rows(x, old, r2, wx, wy, wz, q, start, n, off):
    v, total = neighbours(x, old, wx, wy, wz, start, n, off)
    rows = pl.ds(start, n)
    damped = q[x, rows, :]
    diagonal = DAMPING / jnp.where(damped == 0.0, 1.0, damped)
    return 0.5 * ((r2[x, rows, :] + total) - diagonal * v)


def put_rows(slot, buf, res, rows):
    for r in rows:
        buf[pl.ds(slot[r], 1), :] = res[r : r + 1, :]


def inner_kernel(slot, p_ref, k_ref, r_ref, bl, bh, buf_in, buf, kx, rx, va, vb, vc, wx, wy, wz, q, res):
    del buf_in
    xl, xh, _, _ = edges()
    off = zero_index()
    refs = (p_ref, k_ref, r_ref, bl, bh)
    for a, dst in ((0, va), (1, kx), (2, rx)):
        for e in range(EX) if a < 2 else range(1, EX - 1):
            ref, i = halo_plane(refs, a, e)
            values = keep(plane_ok(e, xl, xh), ref[i])
            dst[e, TOP : TOP + CY, :] = values * 2.0 if a == 2 else values
    z = iota((CY, NZ), 1)

    def prep(x, carry):
        ok = ((x >= W) | xl) & ((x < W + CX) | xh)
        prepare_rows(x, kx, wx, wy, wz, q, TOP, CY, None, ok, z)
        return carry

    lax.fori_loop(1, EX - 1, prep, 0, unroll=2)
    own = pl.ds(TOP, CY)
    wx[EX - 1, own, :] = kx[EX - 1, own, :] + kx[EX - 2, own, :]

    def first(x, carry):
        vb[x, own, :] = sweep_rows(x, va, rx, wx, wy, wz, q, TOP, CY, off)
        return carry

    def second(x, carry):
        vc[x, own, :] = sweep_rows(x, vb, rx, wx, wy, wz, q, TOP, CY, off)
        return carry

    def third(x, carry):
        e = x + W
        res[pl.ds(pl.multiple_of(x * CY, CY), CY), :] = residual_rows(e, vc, rx, wx, wy, wz, q, TOP, CY, off)
        return carry

    lax.fori_loop(1, EX - 1, first, 0, unroll=2)
    lax.fori_loop(2, EX - 2, second, 0, unroll=2)
    lax.fori_loop(0, CX, third, 0, unroll=2)

    def put(i, carry):
        for u in range(48):
            r = i * CY + TOP + u
            buf[pl.ds(slot[r], 1), :] = res[pl.ds(r, 1), :]
        return carry

    lax.fori_loop(0, CX, put, 0)


def rim_kernel(
    slot, sl, sh, kx_in, rx_in, va_in, vb_in, vc_in, wx_in, wy_in, wz_in, q_in, res, buf_in,
    kx, rx, va, vb, vc, wx, wy, wz, q, buf,
):
    del kx_in, rx_in, va_in, vb_in, vc_in, wx_in, wy_in, wz_in, q_in, buf_in
    xl, xh, yl, yh = edges()
    off = zero_index()
    end = TOP + CY
    for e in range(1, EX - 1):
        ok = plane_ok(e, xl, xh)
        low_ok, high_ok = (yl, yh) if ok is None else (yl & ok, yh & ok)
        for i, (dst, n, scale) in enumerate(((va, W, 1.0), (kx, W, 1.0), (rx, W - 1, 2.0))):
            at = W * i
            dst[e, TOP - n : TOP, :] = jnp.where(low_ok, sl[e - 1, at : at + n, :], 0.0) * scale
            dst[e, end : end + n, :] = jnp.where(high_ok, sh[e - 1, at : at + n, :], 0.0) * scale
    for e in (0, EX - 1):
        kx[e, TOP - W : TOP, :] = jnp.zeros((W, NZ), F32)
        kx[e, end : end + W, :] = jnp.zeros((W, NZ), F32)
        va[e, TOP - W : TOP, :] = jnp.zeros((W, NZ), F32)
        va[e, end : end + W, :] = jnp.zeros((W, NZ), F32)
    z, y = iota((8, NZ), 1), iota((8, NZ), 0)
    low_rows = (y >= 2) | yl
    high_rows = (y < 6) | yh

    def prep(x, carry):
        ok = ((x >= W) | xl) & ((x < W + CX) | xh)
        prepare_rows(x, kx, wx, wy, wz, q, off + (TOP - 2), 8, None, low_rows & ok, z)
        prepare_rows(x, kx, wx, wy, wz, q, off + (end - 6), 8, off + (end - 5), high_rows & ok, z)
        return carry

    lax.fori_loop(1, EX - 1, prep, 0, unroll=4)
    for start in (TOP - 2, end - 6):
        rows = pl.ds(off + start, 8)
        wx[EX - 1, rows, :] = kx[EX - 1, rows, :] + kx[EX - 2, rows, :]

    def first(x, carry):
        for start in (TOP - 2, end - 6):
            vb[x, pl.ds(off + start, 8), :] = sweep_rows(x, va, rx, wx, wy, wz, q, off + start, 8, 0)
        return carry

    def second(x, carry):
        for start in (TOP - 1, end - 7):
            vc[x, pl.ds(off + start, 8), :] = sweep_rows(x, vb, rx, wx, wy, wz, q, off + start, 8, 0)
        return carry

    lax.fori_loop(1, EX - 1, first, 0, unroll=4)
    lax.fori_loop(2, EX - 2, second, 0, unroll=3)
    for x in range(CX):
        for start in (TOP, end - 8):
            out = residual_rows(x + W, vc, rx, wx, wy, wz, q, start, 8, off)
            for u in range(8):
                buf[pl.ds(slot[x * CY + start - TOP + u], 1), :] = out[u : u + 1]


def parts_of(x):
    a = x.astype(BF16)
    rest = x - a.astype(F32)
    b = rest.astype(BF16)
    return a, b, (rest - b.astype(F32)).astype(BF16)


def coarse_kernel(owners, data, leak_ref, link_ref, back, hot):
    rows = owners * BLOCK
    groups = -(-owners // 3)
    number = (iota((CR, 128), 0) + 1).astype(F32)
    total = jnp.zeros((CR, NZ), F32)
    bases = []
    for g in range(groups):
        base = g * TRIO
        names = [data[base + t * BLOCK + CAP : base + (t + 1) * BLOCK, :] for t in range(min(3, owners - 3 * g))]
        name = names[0]
        for more in names[1:]:
            name = name + more
        if base + 128 > rows:
            name = pltpu.roll(jnp.broadcast_to(name, (8, 128)), base - (rows - 128), 1)[0:1]
            base = rows - 128
        bases.append(base)
        one_hot = jnp.where(number == name, 1.0, 0.0).astype(BF16)
        hot[g] = one_hot
        for part in parts_of(data[base : base + 128, :]):
            total = total + jnp.dot(one_hot, part, preferred_element_type=F32)

    z = iota((CR, NZ), 1)
    link = link_ref[...]
    inner = jnp.where(z == NZ - 1, 0.0, link)
    below = pltpu.roll(inner, 1, 1)
    w = DAMPING / (leak_ref[...] + link + below)
    u = w * total
    for _ in range(2):
        u = (1.0 - DAMPING) * u + w * (total + inner * pltpu.roll(u, NZ - 1, 1) + pltpu.roll(inner * u, 1, 1))
    pieces = parts_of(u)
    for g in range(groups - 1, -1, -1):
        out = jnp.zeros((128, NZ), F32)
        for part in pieces:
            out = out + lax.dot_general(hot[g], part, (((0,), (0,)), ((), ())), preferred_element_type=F32)
        if g == groups - 1:
            back[bases[g] : bases[g] + 128, :] = out
        else:
            back[bases[g] : bases[g] + TRIO, :] = out[0:TRIO]


EDGE = (0, 1, CX - 2, CX - 1)


def edge_kernel(slot, back, vc, to_high, to_low):
    for i, x in enumerate(EDGE):
        dst = to_low if i < 2 else to_high
        for y in range(CY):
            dst[i % 2, y : y + 1, :] = back[pl.ds(slot[x * CY + y], 1), :] + vc[x + W, TOP + y : TOP + y + 1, :]


def body_kernel(slot, back, vc, to_high, to_low, vd):
    for i, x in enumerate(EDGE):
        vd[x + W, TOP : TOP + CY, :] = (to_low if i < 2 else to_high)[i % 2]

    def plane(x, carry):
        for y in range(CY):
            row = back[pl.ds(slot[x * CY + y], 1), :] + vc[x + W, TOP + y : TOP + y + 1, :]
            vd[x + W, TOP + y : TOP + y + 1, :] = row
        return carry

    lax.fori_loop(2, CX - 2, plane, 0)


def last_inner_kernel(vd_in, bl, bh, rx, wx, wy, wz, q, vd, ve, out):
    del vd_in
    xl, xh, _, _ = edges()
    off = zero_index()
    own = pl.ds(TOP, CY)
    for e in (1, 2):
        vd[e, own, :] = keep(xl, bl[e - 1])
        vd[e + CX + 2, own, :] = keep(xh, bh[e - 1])

    def first(x, carry):
        ve[x, own, :] = sweep_rows(x, vd, rx, wx, wy, wz, q, TOP, CY, off)
        return carry

    def second(x, carry):
        out[x] = sweep_rows(x + W, ve, rx, wx, wy, wz, q, TOP, CY, off)
        return carry

    lax.fori_loop(2, EX - 2, first, 0, unroll=2)
    lax.fori_loop(0, CX, second, 0, unroll=2)


def last_rim_kernel(sl, sh, vd_in, ve_in, inner, rx, wx, wy, wz, q, vd, ve, out):
    del vd_in, ve_in
    xl, xh, yl, yh = edges()
    off = zero_index()
    end = TOP + CY
    for e in range(1, EX - 1):
        if 2 <= e < EX - 2:
            ok = plane_ok(e, xl, xh)
            low_ok, high_ok = (yl, yh) if ok is None else (yl & ok, yh & ok)
            vd[e, TOP - 2 : TOP, :] = jnp.where(low_ok, sl[e - 2], 0.0)
            vd[e, end : end + 2, :] = jnp.where(high_ok, sh[e - 2], 0.0)
        else:
            vd[e, TOP - 2 : TOP, :] = jnp.zeros((2, NZ), F32)
            vd[e, end : end + 2, :] = jnp.zeros((2, NZ), F32)

    def first(x, carry):
        for start in (TOP - 1, end - 7):
            ve[x, pl.ds(off + start, 8), :] = sweep_rows(x, vd, rx, wx, wy, wz, q, off + start, 8, 0)
        return carry

    lax.fori_loop(2, EX - 2, first, 0, unroll=3)

    def second(x, carry):
        out[x, 8 : CY - 8, :] = inner[x, 8 : CY - 8, :]
        for start in (TOP, end - 8):
            out[x, start - TOP : start - TOP + 8, :] = sweep_rows(x + W, ve, rx, wx, wy, wz, q, start, 8, off)
        return carry

    lax.fori_loop(0, CX, second, 0, unroll=4)


def ring(axis, step):
    n = lax.axis_size(axis)
    return [(i, (i + step) % n) for i in range(n)]


def from_both(axis, to_high, to_low):
    return lax.ppermute(to_high, axis, ring(axis, 1)), lax.ppermute(to_low, axis, ring(axis, -1))


EXT = ((EX, EY, NZ), F32)


def per_device(pressure, rhs, kappa, owner, coarse_row, coarse_leak, coarse_link):
    owners = lax.axis_size("bulk")
    slots = owners * BLOCK
    sent = ((2 * W + W - 1, CY, NZ), F32)
    side = ((EX - 2, 8, NZ), F32)
    to_high, to_low = call(
        send_kernel,
        [sent, sent],
        (pressure, kappa, rhs),
        mib=2,
    )
    bl, bh = from_both("bulk", to_high, to_low)
    slot, buf = call(
        lambda *refs: slot_kernel(owners, *refs),
        [((8, 128), I32), ((slots, NZ), F32)],
        (owner.reshape(8, 128), coarse_row.reshape(8, 128)),
    )
    to_high, to_low = call(side_kernel, [side, side], (pressure, kappa, rhs, bl, bh, slot))
    slot = slot.reshape(CX * CY)
    sl, sh = from_both("slab", to_high, to_low)
    buf, *ext, res = call(
        inner_kernel,
        [((slots, NZ), F32)] + [EXT] * 9 + [((CX * CY, NZ), F32)],
        (slot, pressure, kappa, rhs, bl, bh, buf),
        in_specs=[SMEM] + [VMEM] * 6,
        aliases={6: 0},
        mib=20,
    )
    *ext, buf = call(
        rim_kernel,
        [EXT] * 9 + [((slots, NZ), F32)],
        (slot, sl, sh, *ext, res, buf),
        in_specs=[SMEM] + [VMEM] * 13,
        aliases={**{3 + i: i for i in range(9)}, 13: 9},
        mib=20,
    )
    _, rx, _, _, vc, wx, wy, wz, q = ext
    got = lax.all_to_all(buf.reshape(owners, BLOCK, 1, NZ), "bulk", 0, 0)
    (back,) = call(
        lambda *refs: coarse_kernel(owners, *refs),
        [((slots, NZ), F32)],
        (got.reshape(slots, NZ), coarse_leak[0], coarse_link[0]),
        scratch=[pltpu.VMEM((-(-owners // 3), CR, 128), BF16)],
    )
    back = lax.all_to_all(back.reshape(owners, BLOCK, 1, NZ), "bulk", 0, 0).reshape(slots, NZ)
    to_high, to_low = call(
        edge_kernel, [((2, CY, NZ), F32)] * 2, (slot, back, vc), in_specs=[SMEM, VMEM, VMEM]
    )
    bl, bh = from_both("bulk", to_high, to_low)
    (vd,) = call(
        body_kernel, [EXT], (slot, back, vc, to_high, to_low), in_specs=[SMEM] + [VMEM] * 4
    )

    def rim(lo, hi):
        return jnp.concatenate([bl[1:, lo:hi], vd[W : W + CX, TOP + lo : TOP + hi], bh[:1, lo:hi]], axis=0)

    sl, sh = from_both("slab", rim(CY - 2, CY), rim(0, 2))
    vd, ve, inner = call(
        last_inner_kernel,
        [EXT, EXT, ((CX, CY, NZ), F32)],
        (vd, bl, bh, rx, wx, wy, wz, q),
        aliases={0: 0},
        mib=20,
    )
    _, _, out = call(
        last_rim_kernel,
        [EXT, EXT, ((CX, CY, NZ), F32)],
        (sl, sh, vd, ve, inner, rx, wx, wy, wz, q),
        aliases={2: 0, 3: 1},
        mib=20,
    )
    return out


def solution(mesh):
    return jax.shard_map(
        per_device,
        mesh=mesh,
        in_specs=(
            P("bulk", "slab", None),
            P("bulk", "slab", None),
            P("bulk", "slab", None),
            P("slab", "bulk", None, None),
            P("slab", "bulk", None),
            P("slab", "bulk", None),
            P("slab", "bulk", None),
        ),
        out_specs=P("bulk", "slab", None),
        check_vma=False,
    )
```

```python
import jax
import jax.numpy as jnp
from jax import lax
from jax.experimental import pallas as pl
from jax.experimental.pallas import tpu as pltpu
from jax.sharding import PartitionSpec as P


DAMPING = 0.8
CX, CY, NZ = 16, 64, 128
CR = 128
CAP = 40
BLOCK = CAP + 1
TRIO = 3 * BLOCK
W = 3
TOP = 8
EX, EY = CX + 2 * W, CY + 2 * TOP
F32, BF16, I32 = jnp.float32, jnp.bfloat16, jnp.int32

VMEM = pl.BlockSpec(memory_space=pltpu.VMEM)
SMEM = pl.BlockSpec(memory_space=pltpu.SMEM)


def iota(shape, dim):
    return lax.broadcasted_iota(I32, shape, dim)


def call(kernel, outs, args, in_specs=None, scratch=(), mib=16, aliases=None, out_specs=None):
    return pl.pallas_call(
        kernel,
        out_shape=[jax.ShapeDtypeStruct(s, d) for s, d in outs],
        in_specs=in_specs or [VMEM] * len(args),
        out_specs=out_specs or [VMEM] * len(outs),
        scratch_shapes=list(scratch),
        input_output_aliases=aliases or {},
        compiler_params=pltpu.CompilerParams(vmem_limit_bytes=mib << 20),
    )(*args)


def slot_kernel(owners, own_ref, row_ref, slot_ref, buf_ref):
    shift = lax.rem(lax.axis_index("bulk"), 3) * BLOCK
    before = (iota((128, 128), 0) < iota((128, 128), 1)).astype(BF16)
    owner_of = iota((owners, 128), 0)
    lane_of = iota((128, 128), 0)
    seen = jnp.zeros((owners, 1), F32)
    numbers = jnp.zeros((owners, 128), F32)
    for b in range(own_ref.shape[0]):
        own = own_ref[b : b + 1, :]
        mine = owner_of == own
        mine_f = mine.astype(F32)
        count = jnp.dot(mine_f.astype(BF16), before, preferred_element_type=F32) + seen
        rank = jnp.sum(jnp.where(mine, count, 0.0), axis=0, keepdims=True).astype(I32)
        seen = seen + jnp.sum(mine_f, axis=1, keepdims=True)
        slot_ref[b : b + 1, :] = own * BLOCK + rank
        named = jnp.where(lane_of == rank + shift, (row_ref[b : b + 1, :] + 1).astype(F32), 0.0)
        numbers = numbers + lax.dot_general(
            mine_f.astype(BF16), named.astype(BF16), (((1,), (1,)), ((), ())), preferred_element_type=F32
        )
    buf_ref[...] = jnp.zeros_like(buf_ref)
    for o in range(owners):
        buf_ref[o * BLOCK + CAP : o * BLOCK + BLOCK, :] = numbers[o : o + 1, :]


def edges():
    b, s = lax.axis_index("bulk"), lax.axis_index("slab")
    return b > 0, b < lax.axis_size("bulk") - 1, s > 0, s < lax.axis_size("slab") - 1


def zero_index():
    return jnp.minimum(lax.axis_index("bulk"), 0)


def keep(ok, values):
    return values if ok is None else jnp.where(ok, values, 0.0)


def plane_ok(e, xl, xh):
    return xl if e < W else (None if e < W + CX else xh)


def send_kernel(p_ref, k_ref, r_ref, to_high, to_low, sems):
    copies = []
    at = 0
    for ref, n in ((p_ref, W), (k_ref, W), (r_ref, W - 1)):
        for src, dst in ((ref.at[pl.ds(CX - n, n)], to_high.at[pl.ds(at, n)]), (ref.at[pl.ds(0, n)], to_low.at[pl.ds(at, n)])):
            copies.append(pltpu.make_async_copy(src, dst, sems.at[len(copies)]))
        at += n
    for copy in copies:
        copy.start()
    for copy in copies:
        copy.wait()


def halo_plane(refs, a, e):
    own, bl, bh = refs[a], refs[3], refs[4]
    if W <= e < W + CX:
        return own, e - W
    at = W * a
    if e < W:
        return bl, at + e - (1 if a == 2 else 0)
    return bh, at + e - W - CX


def side_kernel(p_ref, k_ref, r_ref, bl, bh, done, to_high, to_low):
    del done
    refs = (p_ref, k_ref, r_ref, bl, bh)
    for e in range(1, EX - 1):
        at = 0
        for a, n in ((0, W), (1, W), (2, W - 1)):
            ref, i = halo_plane(refs, a, e)
            to_high[e - 1, at : at + n, :] = ref[i, CY - n : CY, :]
            to_low[e - 1, at : at + n, :] = ref[i, 0:n, :]
            at += n


def prepare_rows(x, k_ref, wx, wy, wz, q, start, n, wy_start, ok, z):
    rows = pl.ds(start, n)
    k = k_ref[x, rows, :]
    low, high = k_ref[x, pl.ds(start - 1, n), :], k_ref[x, pl.ds(start + 1, n), :]
    wxl = k + k_ref[x - 1, rows, :]
    ks = jnp.where(z == 0, 0.0, pltpu.roll(k, 1, 1))
    kn = jnp.where(z == NZ - 1, 0.0, pltpu.roll(k, NZ - 1, 1))
    wzl = k + ks
    diagonal = (wxl + (k + k_ref[x + 1, rows, :])) + ((k + low) + (k + high)) + (wzl + (k + kn))
    ok = ok & (diagonal > 0.0)
    q[x, rows, :] = jnp.where(ok, DAMPING / jnp.where(ok, diagonal, 1.0), 0.0)
    wx[x, rows, :] = wxl
    wz[x, rows, :] = jnp.where(z == 0, 0.0, wzl)
    if wy_start is None:
        wy[x, rows, :] = k + low
    else:
        wy[x, pl.ds(wy_start, n), :] = k_ref[x, pl.ds(wy_start, n), :] + k_ref[x, pl.ds(wy_start - 1, n), :]


def turned(x, v_ref, wz, start, n):
    v = v_ref[x, pl.ds(start, n), :]
    return pltpu.roll(v, 1, 1), pltpu.roll(wz[x, pl.ds(start, n), :] * v, NZ - 1, 1)


def neighbours(x, v_ref, wx, wy, wz, start, n, off, turn):
    rows, below, above = pl.ds(start, n), pl.ds(off + (start - 1), n), pl.ds(off + (start + 1), n)
    total = wx[x, rows, :] * v_ref[x - 1, rows, :] + wx[x + 1, rows, :] * v_ref[x + 1, rows, :]
    total = total + (wy[x, rows, :] * v_ref[x, below, :] + wy[x, above, :] * v_ref[x, above, :])
    return v_ref[x, rows, :], total + (wz[x, rows, :] * turn[0] + turn[1])


def sweep_rows(x, old, r2, wx, wy, wz, q, start, n, off, turn=None):
    turn = turn or turned(x, old, wz, start, n)
    v, total = neighbours(x, old, wx, wy, wz, start, n, off, turn)
    rows = pl.ds(start, n)
    return (1.0 - DAMPING) * v + q[x, rows, :] * (r2[x, rows, :] + total)


def residual_rows(x, old, r2, wx, wy, wz, q, start, n, off, turn=None):
    turn = turn or turned(x, old, wz, start, n)
    v, total = neighbours(x, old, wx, wy, wz, start, n, off, turn)
    rows = pl.ds(start, n)
    damped = q[x, rows, :]
    diagonal = DAMPING / jnp.where(damped == 0.0, 1.0, damped)
    return 0.5 * ((r2[x, rows, :] + total) - diagonal * v)


def planes(first, last, old, wz, body):
    def step(x, turn):
        ahead = turned(x + 1, old, wz, TOP, CY)
        body(x, turn)
        return ahead

    lax.fori_loop(first, last, step, turned(first, old, wz, TOP, CY))


def fill(refs, fields, some, xl, xh):
    for a, dst in enumerate(fields):
        for e in some:
            if a == 2 and e in (0, EX - 1):
                continue
            ref, i = halo_plane(refs, a, e)
            values = keep(plane_ok(e, xl, xh), ref[i])
            dst[e, TOP : TOP + CY, :] = values * 2.0 if a == 2 else values


def inner_steps(ranges, slot, buf, kx, rx, va, vb, vc, wx, wy, wz, q, res, xl, xh):
    off = zero_index()
    z = iota((CY, NZ), 1)
    own = pl.ds(TOP, CY)
    field = (rx, wx, wy, wz, q, TOP, CY, off)

    def prep(x, carry):
        ok = ((x >= W) | xl) & ((x < W + CX) | xh)
        prepare_rows(x, kx, wx, wy, wz, q, TOP, CY, None, ok, z)
        return carry

    def first(x, turn):
        vb[x, own, :] = sweep_rows(x, va, *field, turn)

    def second(x, turn):
        vc[x, own, :] = sweep_rows(x, vb, *field, turn)

    def third(x, turn):
        rows = pl.ds(pl.multiple_of((x - W) * CY, CY), CY)
        res[rows, :] = residual_rows(x, vc, *field, turn)

    def put(x, carry):
        for u in range(CY - 16):
            r = (x - W) * CY + TOP + u
            buf[pl.ds(slot[r], 1), :] = res[pl.ds(r, 1), :]
        return carry

    for lo, hi in ranges[0]:
        lax.fori_loop(lo, hi, prep, 0)
        wx[hi, own, :] = kx[hi, own, :] + kx[hi - 1, own, :]
    for lo, hi in ranges[0]:
        planes(lo, hi, va, wz, first)
    for lo, hi in ranges[1]:
        planes(lo, hi, vb, wz, second)
    for lo, hi in ranges[2]:
        planes(lo, hi, vc, wz, third)
    for lo, hi in ranges[2]:
        lax.fori_loop(lo, hi, put, 0)


def core_kernel(slot, p_ref, k_ref, r_ref, buf_in, buf, kx, rx, va, vb, vc, wx, wy, wz, q, res, done):
    del buf_in
    fill((p_ref, k_ref, r_ref, None, None), (va, kx, rx), range(W, W + CX), None, None)
    a, b = W + 1, W + CX - 1
    ranges = (((a, b),), ((a + 1, b - 1),), ((a + 2, b - 2),))
    inner_steps(ranges, slot, buf, kx, rx, va, vb, vc, wx, wy, wz, q, res, True, True)
    done[...] = jnp.zeros_like(done)


def mid_kernel(slot, bl, bh, *refs):
    buf, kx, rx, va, vb, vc, wx, wy, wz, q, res = refs[11:]
    xl, xh, _, _ = edges()
    halo = [*range(W), *range(W + CX, EX)]
    fill((None, None, None, bl, bh), (va, kx, rx), halo, xl, xh)
    a, b = W + 1, W + CX - 1
    ranges = tuple(((1 + i, a + i), (b - i, EX - 1 - i)) for i in range(3))
    inner_steps(ranges, slot, buf, kx, rx, va, vb, vc, wx, wy, wz, q, res, xl, xh)


def rim_kernel(
    slot_ref, sl, sh, kx_in, rx_in, va_in, vb_in, vc_in, wx_in, wy_in, wz_in, q_in, res, buf_in,
    kx, rx, va, vb, vc, wx, wy, wz, q, buf, slot, sem,
):
    del kx_in, rx_in, va_in, vb_in, vc_in, wx_in, wy_in, wz_in, q_in, buf_in, res
    table = pltpu.make_async_copy(slot_ref, slot, sem)
    table.start()
    xl, xh, yl, yh = edges()
    off = zero_index()
    end = TOP + CY
    for e in range(1, EX - 1):
        ok = plane_ok(e, xl, xh)
        low_ok, high_ok = (yl, yh) if ok is None else (yl & ok, yh & ok)
        for i, (dst, n, scale) in enumerate(((va, W, 1.0), (kx, W, 1.0), (rx, W - 1, 2.0))):
            at = W * i
            dst[e, TOP - n : TOP, :] = jnp.where(low_ok, sl[e - 1, at : at + n, :], 0.0) * scale
            dst[e, end : end + n, :] = jnp.where(high_ok, sh[e - 1, at : at + n, :], 0.0) * scale
    for e in (0, EX - 1):
        kx[e, TOP - W : TOP, :] = jnp.zeros((W, NZ), F32)
        kx[e, end : end + W, :] = jnp.zeros((W, NZ), F32)
        va[e, TOP - W : TOP, :] = jnp.zeros((W, NZ), F32)
        va[e, end : end + W, :] = jnp.zeros((W, NZ), F32)
    z, y = iota((8, NZ), 1), iota((8, NZ), 0)
    low_rows = (y >= 2) | yl
    high_rows = (y < 6) | yh
    field = (rx, wx, wy, wz, q)
    for x in range(1, EX - 1):
        ok = plane_ok(x, xl, xh)
        ok = True if ok is None else ok
        prepare_rows(x, kx, wx, wy, wz, q, off + (TOP - 2), 8, None, low_rows & ok, z)
        prepare_rows(x, kx, wx, wy, wz, q, off + (end - 6), 8, off + (end - 5), high_rows & ok, z)
    for start in (TOP - 2, end - 6):
        rows = pl.ds(off + start, 8)
        wx[EX - 1, rows, :] = kx[EX - 1, rows, :] + kx[EX - 2, rows, :]
    for x in range(1, EX - 1):
        for start in (TOP - 2, end - 6):
            vb[x, pl.ds(off + start, 8), :] = sweep_rows(x, va, *field, off + start, 8, 0)
    for x in range(2, EX - 2):
        for start in (TOP - 1, end - 7):
            vc[x, pl.ds(off + start, 8), :] = sweep_rows(x, vb, *field, off + start, 8, 0)
    table.wait()
    for x in range(CX):
        for start in (TOP, end - 8):
            out = residual_rows(x + W, vc, *field, start, 8, off)
            for u in range(8):
                buf[pl.ds(slot[x * CY + start - TOP + u], 1), :] = out[u : u + 1]


def parts_of(x):
    a = x.astype(BF16)
    rest = x - a.astype(F32)
    b = rest.astype(BF16)
    return a, b, (rest - b.astype(F32)).astype(BF16)


def coarse_kernel(owners, data, leak_ref, link_ref, back, hot):
    rows = owners * BLOCK
    groups = -(-owners // 3)
    number = (iota((CR, 128), 0) + 1).astype(F32)
    total = jnp.zeros((CR, NZ), F32)
    bases = []
    for g in range(groups):
        base = g * TRIO
        names = [data[base + t * BLOCK + CAP : base + (t + 1) * BLOCK, :] for t in range(min(3, owners - 3 * g))]
        name = names[0]
        for more in names[1:]:
            name = name + more
        if base + 128 > rows:
            name = pltpu.roll(jnp.broadcast_to(name, (8, 128)), base - (rows - 128), 1)[0:1]
            base = rows - 128
        bases.append(base)
        one_hot = jnp.where(number == name, 1.0, 0.0).astype(BF16)
        hot[g] = one_hot
        for part in parts_of(data[base : base + 128, :]):
            total = total + jnp.dot(one_hot, part, preferred_element_type=F32)

    z = iota((CR, NZ), 1)
    link = link_ref[...]
    inner = jnp.where(z == NZ - 1, 0.0, link)
    below = pltpu.roll(inner, 1, 1)
    w = DAMPING / (leak_ref[...] + link + below)
    u = w * total
    for _ in range(2):
        u = (1.0 - DAMPING) * u + w * (total + inner * pltpu.roll(u, NZ - 1, 1) + pltpu.roll(inner * u, 1, 1))
    pieces = parts_of(u)
    for g in range(groups - 1, -1, -1):
        out = jnp.zeros((128, NZ), F32)
        for part in pieces:
            out = out + lax.dot_general(hot[g], part, (((0,), (0,)), ((), ())), preferred_element_type=F32)
        if g == groups - 1:
            back[bases[g] : bases[g] + 128, :] = out
        else:
            back[bases[g] : bases[g] + TRIO, :] = out[0:TRIO]


EDGE = (0, 1, CX - 2, CX - 1)


def edge_kernel(slot, back, vc, to_high, to_low):
    for i, x in enumerate(EDGE):
        dst = to_low if i < 2 else to_high
        for y in range(CY):
            dst[i % 2, y : y + 1, :] = back[pl.ds(slot[x * CY + y], 1), :] + vc[x + W, TOP + y : TOP + y + 1, :]


def body_kernel(slot, back, vc, to_high, to_low, vd):
    for i, x in enumerate(EDGE):
        vd[x + W, TOP : TOP + CY, :] = (to_low if i < 2 else to_high)[i % 2]

    def plane(x, carry):
        for y in range(CY):
            row = back[pl.ds(slot[x * CY + y], 1), :] + vc[x + W, TOP + y : TOP + y + 1, :]
            vd[x + W, TOP + y : TOP + y + 1, :] = row
        return carry

    lax.fori_loop(2, CX - 2, plane, 0)


def last_inner_kernel(vd_in, bl, bh, rx, wx, wy, wz, q, vd, ve, out):
    del vd_in
    xl, xh, _, _ = edges()
    off = zero_index()
    own = pl.ds(TOP, CY)
    for e in (1, 2):
        vd[e, own, :] = keep(xl, bl[e - 1])
        vd[e + CX + 2, own, :] = keep(xh, bh[e - 1])

    field = (rx, wx, wy, wz, q, TOP, CY, off)

    def first(x, turn):
        ve[x, own, :] = sweep_rows(x, vd, *field, turn)

    def second(x, turn):
        out[x - W] = sweep_rows(x, ve, *field, turn)

    planes(2, EX - 2, vd, wz, first)
    planes(W, W + CX, ve, wz, second)


def last_rim_kernel(sl, sh, vd_in, ve_in, inner, rx, wx, wy, wz, q, vd, ve, out):
    del vd_in, ve_in
    xl, xh, yl, yh = edges()
    off = zero_index()
    end = TOP + CY
    for e in range(1, EX - 1):
        if 2 <= e < EX - 2:
            ok = plane_ok(e, xl, xh)
            low_ok, high_ok = (yl, yh) if ok is None else (yl & ok, yh & ok)
            vd[e, TOP - 2 : TOP, :] = jnp.where(low_ok, sl[e - 2], 0.0)
            vd[e, end : end + 2, :] = jnp.where(high_ok, sh[e - 2], 0.0)
        else:
            vd[e, TOP - 2 : TOP, :] = jnp.zeros((2, NZ), F32)
            vd[e, end : end + 2, :] = jnp.zeros((2, NZ), F32)

    def first(x, carry):
        for start in (TOP - 1, end - 7):
            ve[x, pl.ds(off + start, 8), :] = sweep_rows(x, vd, rx, wx, wy, wz, q, off + start, 8, 0)
        return carry

    lax.fori_loop(2, EX - 2, first, 0, unroll=3)

    def second(x, carry):
        out[x, 8 : CY - 8, :] = inner[x, 8 : CY - 8, :]
        for start in (TOP, end - 8):
            out[x, start - TOP : start - TOP + 8, :] = sweep_rows(x + W, ve, rx, wx, wy, wz, q, start, 8, off)
        return carry

    lax.fori_loop(0, CX, second, 0, unroll=4)


def ring(axis, step):
    n = lax.axis_size(axis)
    return [(i, (i + step) % n) for i in range(n)]


def from_both(axis, to_high, to_low):
    low = lax.ppermute(to_high, axis, ring(axis, 1))
    high = lax.ppermute(to_low, axis, ring(axis, -1))
    return low, high


EXT = ((EX, EY, NZ), F32)


def cycle(pressure, rhs, kappa, owner, coarse_row, coarse_leak, coarse_link):
    owners = lax.axis_size("bulk")
    slots = owners * BLOCK
    sent = ((2 * W + W - 1, CY, NZ), F32)
    side = ((EX - 2, 8, NZ), F32)
    to_high, to_low = call(
        send_kernel,
        [sent, sent],
        [pltpu.with_memory_space_constraint(f, pltpu.MemorySpace.HBM) for f in (pressure, kappa, rhs)],
        in_specs=[pl.BlockSpec(memory_space=pltpu.MemorySpace.HBM)] * 3,
        scratch=[pltpu.SemaphoreType.DMA((6,))],
        mib=2,
    )
    bl, bh = from_both("bulk", to_high, to_low)
    slot, buf = call(
        lambda *refs: slot_kernel(owners, *refs),
        [((8, 128), I32), ((slots, NZ), F32)],
        (owner.reshape(8, 128), coarse_row.reshape(8, 128)),
    )
    table = slot.reshape(CX * CY)
    work = [((slots, NZ), F32)] + [EXT] * 9 + [((CX * CY, NZ), F32)]
    *core, done = call(
        core_kernel,
        work + [((8, NZ), F32)],
        (table, pressure, kappa, rhs, buf),
        in_specs=[SMEM] + [VMEM] * 4,
        aliases={4: 0},
        mib=20,
    )
    to_high, to_low = call(side_kernel, [side, side], (pressure, kappa, rhs, bl, bh, done))
    sl, sh = from_both("slab", to_high, to_low)
    buf, *ext, res = call(
        mid_kernel,
        work,
        (table, bl, bh, *core),
        in_specs=[SMEM] + [VMEM] * 13,
        aliases={3 + i: i for i in range(11)},
        mib=20,
    )
    *ext, buf = call(
        rim_kernel,
        [EXT] * 9 + [((slots, NZ), F32)],
        (table, sl, sh, *ext, res, buf),
        aliases={**{3 + i: i for i in range(9)}, 13: 9},
        scratch=[pltpu.SMEM((CX * CY,), I32), pltpu.SemaphoreType.DMA],
        mib=20,
    )
    _, rx, _, _, vc, wx, wy, wz, q = ext
    got = lax.all_to_all(buf.reshape(owners, BLOCK, 1, NZ), "bulk", 0, 0)
    (back,) = call(
        lambda *refs: coarse_kernel(owners, *refs),
        [((slots, NZ), F32)],
        (got.reshape(slots, NZ), coarse_leak[0], coarse_link[0]),
        scratch=[pltpu.VMEM((-(-owners // 3), CR, 128), BF16)],
    )
    back = lax.all_to_all(back.reshape(owners, BLOCK, 1, NZ), "bulk", 0, 0).reshape(slots, NZ)
    to_high, to_low = call(
        edge_kernel, [((2, CY, NZ), F32)] * 2, (table, back, vc), in_specs=[SMEM, VMEM, VMEM]
    )
    bl, bh = from_both("bulk", to_high, to_low)
    (vd,) = call(body_kernel, [EXT], (table, back, vc, to_high, to_low), in_specs=[SMEM] + [VMEM] * 4)

    def rim(lo, hi):
        return jnp.concatenate([bl[1:, lo:hi], vd[W : W + CX, TOP + lo : TOP + hi], bh[:1, lo:hi]], axis=0)

    sl, sh = from_both("slab", rim(CY - 2, CY), rim(0, 2))
    vd, ve, inner = call(
        last_inner_kernel,
        [EXT, EXT, ((CX, CY, NZ), F32)],
        (vd, bl, bh, rx, wx, wy, wz, q),
        aliases={0: 0},
        mib=20,
    )
    _, _, out = call(
        last_rim_kernel,
        [EXT, EXT, ((CX, CY, NZ), F32)],
        (sl, sh, vd, ve, inner, rx, wx, wy, wz, q),
        aliases={2: 0, 3: 1},
        mib=20,
    )
    return out


def solution(mesh):
    return jax.shard_map(
        cycle,
        mesh=mesh,
        in_specs=(
            P("bulk", "slab", None),
            P("bulk", "slab", None),
            P("bulk", "slab", None),
            P("slab", "bulk", None, None),
            P("slab", "bulk", None),
            P("slab", "bulk", None),
            P("slab", "bulk", None),
        ),
        out_specs=P("bulk", "slab", None),
        check_vma=False,
    )
```

```python
import jax
import jax.numpy as jnp
from jax import lax
from jax.experimental import pallas as pl
from jax.experimental.pallas import tpu as pltpu
from jax.sharding import PartitionSpec as P


DAMPING = 0.8
CX, CY, NZ = 16, 64, 128
CR = 128
CAP = 40
BLOCK = CAP + 1
TRIO = 3 * BLOCK
W = 3
TOP = 8
EX, EY = CX + 2 * W, CY + 2 * TOP
F32, BF16, I32 = jnp.float32, jnp.bfloat16, jnp.int32

VMEM = pl.BlockSpec(memory_space=pltpu.VMEM)
SMEM = pl.BlockSpec(memory_space=pltpu.SMEM)


def iota(shape, dim):
    return lax.broadcasted_iota(I32, shape, dim)


def call(kernel, outs, args, in_specs=None, scratch=(), mib=16, aliases=None, out_specs=None):
    return pl.pallas_call(
        kernel,
        out_shape=[jax.ShapeDtypeStruct(s, d) for s, d in outs],
        in_specs=in_specs or [VMEM] * len(args),
        out_specs=out_specs or [VMEM] * len(outs),
        scratch_shapes=list(scratch),
        input_output_aliases=aliases or {},
        compiler_params=pltpu.CompilerParams(vmem_limit_bytes=mib << 20),
    )(*args)


def slot_kernel(owners, own_ref, row_ref, slot_ref, buf_ref):
    shift = lax.rem(lax.axis_index("bulk"), 3) * BLOCK
    before = (iota((128, 128), 0) < iota((128, 128), 1)).astype(BF16)
    owner_of = iota((owners, 128), 0)
    lane_of = iota((128, 128), 0)
    seen = jnp.zeros((owners, 1), F32)
    numbers = jnp.zeros((owners, 128), F32)
    for b in range(own_ref.shape[0]):
        own = own_ref[b : b + 1, :]
        mine = owner_of == own
        mine_f = mine.astype(F32)
        count = jnp.dot(mine_f.astype(BF16), before, preferred_element_type=F32) + seen
        rank = jnp.sum(jnp.where(mine, count, 0.0), axis=0, keepdims=True).astype(I32)
        seen = seen + jnp.sum(mine_f, axis=1, keepdims=True)
        slot_ref[b : b + 1, :] = own * BLOCK + rank
        named = jnp.where(lane_of == rank + shift, (row_ref[b : b + 1, :] + 1).astype(F32), 0.0)
        numbers = numbers + lax.dot_general(
            mine_f.astype(BF16), named.astype(BF16), (((1,), (1,)), ((), ())), preferred_element_type=F32
        )
    buf_ref[...] = jnp.zeros_like(buf_ref)
    for o in range(owners):
        buf_ref[o * BLOCK + CAP : o * BLOCK + BLOCK, :] = numbers[o : o + 1, :]


def edges():
    b, s = lax.axis_index("bulk"), lax.axis_index("slab")
    return b > 0, b < lax.axis_size("bulk") - 1, s > 0, s < lax.axis_size("slab") - 1


def zero_index():
    return jnp.minimum(lax.axis_index("bulk"), 0)


def keep(ok, values):
    return values if ok is None else jnp.where(ok, values, 0.0)


def plane_ok(e, xl, xh):
    return xl if e < W else (None if e < W + CX else xh)


def send_kernel(p_ref, k_ref, r_ref, to_high, to_low, sems):
    copies = []
    at = 0
    for ref, n in ((p_ref, W), (k_ref, W), (r_ref, W - 1)):
        for src, dst in ((ref.at[pl.ds(CX - n, n)], to_high.at[pl.ds(at, n)]), (ref.at[pl.ds(0, n)], to_low.at[pl.ds(at, n)])):
            copies.append(pltpu.make_async_copy(src, dst, sems.at[len(copies)]))
        at += n
    for copy in copies:
        copy.start()
    for copy in copies:
        copy.wait()


def halo_plane(refs, a, e):
    own, bl, bh = refs[a], refs[3], refs[4]
    if W <= e < W + CX:
        return own, e - W
    at = W * a
    if e < W:
        return bl, at + e - (1 if a == 2 else 0)
    return bh, at + e - W - CX


def side_kernel(p_ref, k_ref, r_ref, bl, bh, done, to_high, to_low):
    del done
    refs = (p_ref, k_ref, r_ref, bl, bh)
    for e in range(1, EX - 1):
        at = 0
        for a, n in ((0, W), (1, W), (2, W - 1)):
            ref, i = halo_plane(refs, a, e)
            to_high[e - 1, at : at + n, :] = ref[i, CY - n : CY, :]
            to_low[e - 1, at : at + n, :] = ref[i, 0:n, :]
            at += n


def prepare_rows(x, k_ref, wx, wy, wz, q, start, n, wy_start, ok, z):
    rows = pl.ds(start, n)
    k = k_ref[x, rows, :]
    low, high = k_ref[x, pl.ds(start - 1, n), :], k_ref[x, pl.ds(start + 1, n), :]
    wxl = k + k_ref[x - 1, rows, :]
    ks = jnp.where(z == 0, 0.0, pltpu.roll(k, 1, 1))
    kn = jnp.where(z == NZ - 1, 0.0, pltpu.roll(k, NZ - 1, 1))
    wzl = k + ks
    diagonal = (wxl + (k + k_ref[x + 1, rows, :])) + ((k + low) + (k + high)) + (wzl + (k + kn))
    ok = ok & (diagonal > 0.0)
    q[x, rows, :] = jnp.where(ok, DAMPING / jnp.where(ok, diagonal, 1.0), 0.0)
    wx[x, rows, :] = wxl
    wz[x, rows, :] = jnp.where(z == 0, 0.0, wzl)
    if wy_start is None:
        wy[x, rows, :] = k + low
    else:
        wy[x, pl.ds(wy_start, n), :] = k_ref[x, pl.ds(wy_start, n), :] + k_ref[x, pl.ds(wy_start - 1, n), :]


def neighbours(x, v_ref, wx, wy, wz, start, n, off):
    rows, below, above = pl.ds(start, n), pl.ds(off + (start - 1), n), pl.ds(off + (start + 1), n)
    v = v_ref[x, rows, :]
    wzl = wz[x, rows, :]
    total = wx[x, rows, :] * v_ref[x - 1, rows, :] + wx[x + 1, rows, :] * v_ref[x + 1, rows, :]
    total = total + (wy[x, rows, :] * v_ref[x, below, :] + wy[x, above, :] * v_ref[x, above, :])
    return v, total + (wzl * pltpu.roll(v, 1, 1) + pltpu.roll(wzl * v, NZ - 1, 1))


def sweep_rows(x, old, r2, wx, wy, wz, q, start, n, off):
    v, total = neighbours(x, old, wx, wy, wz, start, n, off)
    rows = pl.ds(start, n)
    return (1.0 - DAMPING) * v + q[x, rows, :] * (r2[x, rows, :] + total)


def residual_rows(x, old, r2, wx, wy, wz, q, start, n, off):
    v, total = neighbours(x, old, wx, wy, wz, start, n, off)
    rows = pl.ds(start, n)
    damped = q[x, rows, :]
    diagonal = DAMPING / jnp.where(damped == 0.0, 1.0, damped)
    return 0.5 * ((r2[x, rows, :] + total) - diagonal * v)


def fill(refs, fields, some, xl, xh):
    for a, dst in enumerate(fields):
        for e in some:
            if a == 2 and e in (0, EX - 1):
                continue
            ref, i = halo_plane(refs, a, e)
            values = keep(plane_ok(e, xl, xh), ref[i])
            dst[e, TOP : TOP + CY, :] = values * 2.0 if a == 2 else values


def inner_steps(ranges, slot, buf, kx, rx, va, vb, vc, wx, wy, wz, q, res, xl, xh):
    off = zero_index()
    z = iota((CY, NZ), 1)
    own = pl.ds(TOP, CY)
    field = (rx, wx, wy, wz, q, TOP, CY, off)

    for lo, hi in ranges[0]:
        for x in range(lo, hi):
            ok = plane_ok(x, xl, xh)
            prepare_rows(x, kx, wx, wy, wz, q, TOP, CY, None, True if ok is None else ok, z)
        wx[hi, own, :] = kx[hi, own, :] + kx[hi - 1, own, :]
    for lo, hi in ranges[0]:
        for x in range(lo, hi):
            vb[x, own, :] = sweep_rows(x, va, *field)
    for lo, hi in ranges[1]:
        for x in range(lo, hi):
            vc[x, own, :] = sweep_rows(x, vb, *field)
    for lo, hi in ranges[2]:
        for x in range(lo, hi):
            at = (x - W) * CY
            res[at : at + CY, :] = residual_rows(x, vc, *field)
            for r in range(at + TOP, at + CY - TOP):
                buf[pl.ds(slot[r], 1), :] = res[r : r + 1, :]


def core_kernel(slot, p_ref, k_ref, r_ref, buf_in, buf, kx, rx, va, vb, vc, wx, wy, wz, q, res, done):
    del buf_in
    fill((p_ref, k_ref, r_ref, None, None), (va, kx, rx), range(W, W + CX), None, None)
    a, b = W + 1, W + CX - 1
    ranges = (((a, b),), ((a + 1, b - 1),), ((a + 2, b - 2),))
    inner_steps(ranges, slot, buf, kx, rx, va, vb, vc, wx, wy, wz, q, res, True, True)
    done[...] = jnp.zeros_like(done)


def mid_kernel(slot, bl, bh, *refs):
    buf, kx, rx, va, vb, vc, wx, wy, wz, q, res = refs[11:]
    xl, xh, _, _ = edges()
    halo = [*range(W), *range(W + CX, EX)]
    fill((None, None, None, bl, bh), (va, kx, rx), halo, xl, xh)
    a, b = W + 1, W + CX - 1
    ranges = tuple(((1 + i, a + i), (b - i, EX - 1 - i)) for i in range(3))
    inner_steps(ranges, slot, buf, kx, rx, va, vb, vc, wx, wy, wz, q, res, xl, xh)


def rim_kernel(
    slot_ref, sl, sh, kx_in, rx_in, va_in, vb_in, vc_in, wx_in, wy_in, wz_in, q_in, res, buf_in,
    kx, rx, va, vb, vc, wx, wy, wz, q, buf, slot, sem,
):
    del kx_in, rx_in, va_in, vb_in, vc_in, wx_in, wy_in, wz_in, q_in, buf_in, res
    table = pltpu.make_async_copy(slot_ref, slot, sem)
    table.start()
    xl, xh, yl, yh = edges()
    off = zero_index()
    end = TOP + CY
    for e in range(1, EX - 1):
        ok = plane_ok(e, xl, xh)
        low_ok, high_ok = (yl, yh) if ok is None else (yl & ok, yh & ok)
        for i, (dst, n, scale) in enumerate(((va, W, 1.0), (kx, W, 1.0), (rx, W - 1, 2.0))):
            at = W * i
            dst[e, TOP - n : TOP, :] = jnp.where(low_ok, sl[e - 1, at : at + n, :], 0.0) * scale
            dst[e, end : end + n, :] = jnp.where(high_ok, sh[e - 1, at : at + n, :], 0.0) * scale
    for e in (0, EX - 1):
        kx[e, TOP - W : TOP, :] = jnp.zeros((W, NZ), F32)
        kx[e, end : end + W, :] = jnp.zeros((W, NZ), F32)
        va[e, TOP - W : TOP, :] = jnp.zeros((W, NZ), F32)
        va[e, end : end + W, :] = jnp.zeros((W, NZ), F32)
    z, y = iota((8, NZ), 1), iota((8, NZ), 0)
    low_rows = (y >= 2) | yl
    high_rows = (y < 6) | yh
    field = (rx, wx, wy, wz, q)
    for x in range(1, EX - 1):
        ok = plane_ok(x, xl, xh)
        ok = True if ok is None else ok
        prepare_rows(x, kx, wx, wy, wz, q, off + (TOP - 2), 8, None, low_rows & ok, z)
        prepare_rows(x, kx, wx, wy, wz, q, off + (end - 6), 8, off + (end - 5), high_rows & ok, z)
    for start in (TOP - 2, end - 6):
        rows = pl.ds(off + start, 8)
        wx[EX - 1, rows, :] = kx[EX - 1, rows, :] + kx[EX - 2, rows, :]
    for x in range(1, EX - 1):
        for start in (TOP - 2, end - 6):
            vb[x, pl.ds(off + start, 8), :] = sweep_rows(x, va, *field, off + start, 8, 0)
    for x in range(2, EX - 2):
        for start in (TOP - 1, end - 7):
            vc[x, pl.ds(off + start, 8), :] = sweep_rows(x, vb, *field, off + start, 8, 0)
    table.wait()
    for x in range(CX):
        for start in (TOP, end - 8):
            out = residual_rows(x + W, vc, *field, start, 8, off)
            for u in range(8):
                buf[pl.ds(slot[x * CY + start - TOP + u], 1), :] = out[u : u + 1]


def parts_of(x):
    a = x.astype(BF16)
    rest = x - a.astype(F32)
    b = rest.astype(BF16)
    return a, b, (rest - b.astype(F32)).astype(BF16)


def coarse_kernel(owners, data, leak_ref, link_ref, back, hot, parts):
    rows = owners * BLOCK
    groups = -(-owners // 3)
    pairs = -(-groups // 2)
    number = (iota((CR, 128), 0) + 1).astype(F32)
    total = jnp.zeros((CR, 3 * NZ), F32)
    bases = []
    for g in range(groups):
        base = g * TRIO
        names = [data[base + t * BLOCK + CAP : base + (t + 1) * BLOCK, :] for t in range(min(3, owners - 3 * g))]
        name = names[0]
        for more in names[1:]:
            name = name + more
        if base + 128 > rows:
            name = pltpu.roll(jnp.broadcast_to(name, (8, 128)), base - (rows - 128), 1)[0:1]
            base = rows - 128
        bases.append(base)
        at = g % 2 * 128
        hot[g // 2, :, at : at + 128] = jnp.where(number == name, 1.0, 0.0).astype(BF16)
        for i, part in enumerate(parts_of(data[base : base + 128, :])):
            parts[g // 2, at : at + 128, i * NZ : (i + 1) * NZ] = part
    if groups % 2:
        hot[pairs - 1, :, 128:] = jnp.zeros((CR, 128), BF16)
        parts[pairs - 1, 128:, :] = jnp.zeros((128, 3 * NZ), BF16)
    for p in range(pairs):
        total = total + jnp.dot(hot[p], parts[p], preferred_element_type=F32)
    total = total[:, 0:NZ] + (total[:, NZ : 2 * NZ] + total[:, 2 * NZ :])

    z = iota((CR, NZ), 1)
    link = link_ref[...]
    inner = jnp.where(z == NZ - 1, 0.0, link)
    below = pltpu.roll(inner, 1, 1)
    w = DAMPING / (leak_ref[...] + link + below)
    u = w * total
    for _ in range(2):
        u = (1.0 - DAMPING) * u + w * (total + inner * pltpu.roll(u, NZ - 1, 1) + pltpu.roll(inner * u, 1, 1))
    pieces = jnp.concatenate(parts_of(u), axis=1)
    for p in range(pairs - 1, -1, -1):
        out = lax.dot_general(hot[p], pieces, (((0,), (0,)), ((), ())), preferred_element_type=F32)
        out = out[:, 0:NZ] + (out[:, NZ : 2 * NZ] + out[:, 2 * NZ :])
        for g in (2 * p + 1, 2 * p):
            if g < groups:
                n = 128 if g == groups - 1 else TRIO
                at = g % 2 * 128
                back[bases[g] : bases[g] + n, :] = out[at : at + n]


EDGE = (0, 1, CX - 2, CX - 1)


def edge_kernel(slot, back, vc, to_high, to_low):
    for i, x in enumerate(EDGE):
        dst = to_low if i < 2 else to_high
        for y in range(CY):
            dst[i % 2, y : y + 1, :] = back[pl.ds(slot[x * CY + y], 1), :] + vc[x + W, TOP + y : TOP + y + 1, :]


def body_kernel(slot, back, vc, to_high, to_low, vd):
    for i, x in enumerate(EDGE):
        vd[x + W, TOP : TOP + CY, :] = (to_low if i < 2 else to_high)[i % 2]

    def plane(x, carry):
        for y in range(CY):
            row = back[pl.ds(slot[x * CY + y], 1), :] + vc[x + W, TOP + y : TOP + y + 1, :]
            vd[x + W, TOP + y : TOP + y + 1, :] = row
        return carry

    lax.fori_loop(2, CX - 2, plane, 0)


def last_inner_kernel(vd_in, bl, bh, rx, wx, wy, wz, q, vd, ve, out):
    del vd_in
    xl, xh, _, _ = edges()
    off = zero_index()
    own = pl.ds(TOP, CY)
    for e in (1, 2):
        vd[e, own, :] = keep(xl, bl[e - 1])
        vd[e + CX + 2, own, :] = keep(xh, bh[e - 1])

    field = (rx, wx, wy, wz, q, TOP, CY, off)

    for x in range(2, EX - 2):
        ve[x, own, :] = sweep_rows(x, vd, *field)
    for x in range(CX):
        out[x] = sweep_rows(x + W, ve, *field)


def last_rim_kernel(sl, sh, vd_in, ve_in, inner, rx, wx, wy, wz, q, vd, ve, out):
    del vd_in, ve_in
    xl, xh, yl, yh = edges()
    off = zero_index()
    end = TOP + CY
    for e in range(1, EX - 1):
        if 2 <= e < EX - 2:
            ok = plane_ok(e, xl, xh)
            low_ok, high_ok = (yl, yh) if ok is None else (yl & ok, yh & ok)
            vd[e, TOP - 2 : TOP, :] = jnp.where(low_ok, sl[e - 2], 0.0)
            vd[e, end : end + 2, :] = jnp.where(high_ok, sh[e - 2], 0.0)
        else:
            vd[e, TOP - 2 : TOP, :] = jnp.zeros((2, NZ), F32)
            vd[e, end : end + 2, :] = jnp.zeros((2, NZ), F32)

    field = (rx, wx, wy, wz, q)
    for x in range(2, EX - 2):
        for start in (TOP - 1, end - 7):
            ve[x, pl.ds(off + start, 8), :] = sweep_rows(x, vd, *field, off + start, 8, 0)
    for x in range(CX):
        out[x, 8 : CY - 8, :] = inner[x, 8 : CY - 8, :]
        for start in (TOP, end - 8):
            out[x, start - TOP : start - TOP + 8, :] = sweep_rows(x + W, ve, *field, start, 8, off)


def ring(axis, step):
    n = lax.axis_size(axis)
    return [(i, (i + step) % n) for i in range(n)]


def from_both(axis, to_high, to_low):
    low = lax.ppermute(to_high, axis, ring(axis, 1))
    high = lax.ppermute(to_low, axis, ring(axis, -1))
    return low, high


EXT = ((EX, EY, NZ), F32)


def cycle(pressure, rhs, kappa, owner, coarse_row, coarse_leak, coarse_link):
    owners = lax.axis_size("bulk")
    slots = owners * BLOCK
    sent = ((2 * W + W - 1, CY, NZ), F32)
    side = ((EX - 2, 8, NZ), F32)
    to_high, to_low = call(
        send_kernel,
        [sent, sent],
        [pltpu.with_memory_space_constraint(f, pltpu.MemorySpace.HBM) for f in (pressure, kappa, rhs)],
        in_specs=[pl.BlockSpec(memory_space=pltpu.MemorySpace.HBM)] * 3,
        scratch=[pltpu.SemaphoreType.DMA((6,))],
        mib=2,
    )
    bl, bh = from_both("bulk", to_high, to_low)
    slot, buf = call(
        lambda *refs: slot_kernel(owners, *refs),
        [((8, 128), I32), ((slots, NZ), F32)],
        (owner.reshape(8, 128), coarse_row.reshape(8, 128)),
    )
    table = slot.reshape(CX * CY)
    work = [((slots, NZ), F32)] + [EXT] * 9 + [((CX * CY, NZ), F32)]
    *core, done = call(
        core_kernel,
        work + [((8, NZ), F32)],
        (table, pressure, kappa, rhs, buf),
        in_specs=[SMEM] + [VMEM] * 4,
        aliases={4: 0},
        mib=20,
    )
    to_high, to_low = call(side_kernel, [side, side], (pressure, kappa, rhs, bl, bh, done))
    sl, sh = from_both("slab", to_high, to_low)
    buf, *ext, res = call(
        mid_kernel,
        work,
        (table, bl, bh, *core),
        in_specs=[SMEM] + [VMEM] * 13,
        aliases={3 + i: i for i in range(11)},
        mib=20,
    )
    *ext, buf = call(
        rim_kernel,
        [EXT] * 9 + [((slots, NZ), F32)],
        (table, sl, sh, *ext, res, buf),
        aliases={**{3 + i: i for i in range(9)}, 13: 9},
        scratch=[pltpu.SMEM((CX * CY,), I32), pltpu.SemaphoreType.DMA],
        mib=20,
    )
    _, rx, _, _, vc, wx, wy, wz, q = ext
    got = lax.all_to_all(buf.reshape(owners, BLOCK, 1, NZ), "bulk", 0, 0)
    (back,) = call(
        lambda *refs: coarse_kernel(owners, *refs),
        [((slots, NZ), F32)],
        (got.reshape(slots, NZ), coarse_leak[0], coarse_link[0]),
        scratch=[pltpu.VMEM((-(-owners // 6), CR, 256), BF16), pltpu.VMEM((-(-owners // 6), 256, 3 * NZ), BF16)],
    )
    back = lax.all_to_all(back.reshape(owners, BLOCK, 1, NZ), "bulk", 0, 0).reshape(slots, NZ)
    to_high, to_low = call(
        edge_kernel, [((2, CY, NZ), F32)] * 2, (table, back, vc), in_specs=[SMEM, VMEM, VMEM]
    )
    bl, bh = from_both("bulk", to_high, to_low)
    (vd,) = call(body_kernel, [EXT], (table, back, vc, to_high, to_low), in_specs=[SMEM] + [VMEM] * 4)

    def rim(lo, hi):
        return jnp.concatenate([bl[1:, lo:hi], vd[W : W + CX, TOP + lo : TOP + hi], bh[:1, lo:hi]], axis=0)

    sl, sh = from_both("slab", rim(CY - 2, CY), rim(0, 2))
    vd, ve, inner = call(
        last_inner_kernel,
        [EXT, EXT, ((CX, CY, NZ), F32)],
        (vd, bl, bh, rx, wx, wy, wz, q),
        aliases={0: 0},
        mib=20,
    )
    _, _, out = call(
        last_rim_kernel,
        [EXT, EXT, ((CX, CY, NZ), F32)],
        (sl, sh, vd, ve, inner, rx, wx, wy, wz, q),
        aliases={2: 0, 3: 1},
        mib=20,
    )
    return out


def solution(mesh):
    return jax.shard_map(
        cycle,
        mesh=mesh,
        in_specs=(
            P("bulk", "slab", None),
            P("bulk", "slab", None),
            P("bulk", "slab", None),
            P("slab", "bulk", None, None),
            P("slab", "bulk", None),
            P("slab", "bulk", None),
            P("slab", "bulk", None),
        ),
        out_specs=P("bulk", "slab", None),
        check_vma=False,
    )
```

```python
import jax
import jax.numpy as jnp
from jax import lax
from jax.experimental import pallas as pl
from jax.experimental.pallas import tpu as pltpu
from jax.sharding import PartitionSpec as P


DAMPING = 0.8
CX, CY, NZ = 16, 64, 128
CR = 128
CAP = 40
BLOCK = CAP + 1
TRIO = 3 * BLOCK
W = 3
TOP = 8
EX, EY = CX + 2 * W, CY + 2 * TOP
F32, BF16, I32 = jnp.float32, jnp.bfloat16, jnp.int32

VMEM = pl.BlockSpec(memory_space=pltpu.VMEM)
SMEM = pl.BlockSpec(memory_space=pltpu.SMEM)


def iota(shape, dim):
    return lax.broadcasted_iota(I32, shape, dim)


def call(kernel, outs, args, in_specs=None, scratch=(), mib=16, aliases=None, out_specs=None):
    return pl.pallas_call(
        kernel,
        out_shape=[jax.ShapeDtypeStruct(s, d) for s, d in outs],
        in_specs=in_specs or [VMEM] * len(args),
        out_specs=out_specs or [VMEM] * len(outs),
        scratch_shapes=list(scratch),
        input_output_aliases=aliases or {},
        compiler_params=pltpu.CompilerParams(vmem_limit_bytes=mib << 20),
    )(*args)


def slot_kernel(owners, own_ref, row_ref, slot_ref, buf_ref):
    shift = lax.rem(lax.axis_index("bulk"), 3) * BLOCK
    before = (iota((128, 128), 0) < iota((128, 128), 1)).astype(BF16)
    owner_of = iota((owners, 128), 0)
    lane_of = iota((128, 128), 0)
    seen = jnp.zeros((owners, 1), F32)
    numbers = jnp.zeros((owners, 128), F32)
    for b in range(own_ref.shape[0]):
        own = own_ref[b : b + 1, :]
        mine = owner_of == own
        mine_f = mine.astype(F32)
        count = jnp.dot(mine_f.astype(BF16), before, preferred_element_type=F32) + seen
        rank = jnp.sum(jnp.where(mine, count, 0.0), axis=0, keepdims=True).astype(I32)
        seen = seen + jnp.sum(mine_f, axis=1, keepdims=True)
        slot_ref[b : b + 1, :] = own * BLOCK + rank
        named = jnp.where(lane_of == rank + shift, (row_ref[b : b + 1, :] + 1).astype(F32), 0.0)
        numbers = numbers + lax.dot_general(
            mine_f.astype(BF16), named.astype(BF16), (((1,), (1,)), ((), ())), preferred_element_type=F32
        )
    buf_ref[...] = jnp.zeros_like(buf_ref)
    for o in range(owners):
        buf_ref[o * BLOCK + CAP : o * BLOCK + BLOCK, :] = numbers[o : o + 1, :]


def edges():
    b, s = lax.axis_index("bulk"), lax.axis_index("slab")
    return b > 0, b < lax.axis_size("bulk") - 1, s > 0, s < lax.axis_size("slab") - 1


def zero_index():
    return jnp.minimum(lax.axis_index("bulk"), 0)


def keep(ok, values):
    return values if ok is None else jnp.where(ok, values, 0.0)


def plane_ok(e, xl, xh):
    return xl if e < W else (None if e < W + CX else xh)


def is_odd():
    return lax.rem(lax.axis_index("bulk"), 2) == 1


def send_kernel(p_ref, k_ref, r_ref, to_o, to_e, sems):
    odd = is_odd()
    copies = []
    at = 0
    for ref, n in ((p_ref, W), (k_ref, W), (r_ref, W - 1)):
        for dst, high in ((to_o, odd), (to_e, jnp.logical_not(odd))):
            src = ref.at[pl.ds(jnp.where(high, CX - n, 0), n)]
            copies.append(pltpu.make_async_copy(src, dst.at[pl.ds(at, n)], sems.at[len(copies)]))
        at += n
    for copy in copies:
        copy.start()
    for copy in copies:
        copy.wait()


def halo_plane(refs, a, e, rows):
    own, from_o, from_e, odd = refs[a], refs[3], refs[4], refs[5]
    if W <= e < W + CX:
        return own[e - W, rows, :]
    low = e < W
    i = W * a + (e - (1 if a == 2 else 0) if low else e - W - CX)
    of_o, of_e = from_o[i, rows, :], from_e[i, rows, :]
    return jnp.where(odd, of_e, of_o) if low else jnp.where(odd, of_o, of_e)


def side_kernel(p_ref, k_ref, r_ref, from_o, from_e, done, to_high, to_low):
    del done
    refs = (p_ref, k_ref, r_ref, from_o, from_e, is_odd())
    for e in range(1, EX - 1):
        at = 0
        for a, n in ((0, W), (1, W), (2, W - 1)):
            to_high[e - 1, at : at + n, :] = halo_plane(refs, a, e, slice(CY - n, CY))
            to_low[e - 1, at : at + n, :] = halo_plane(refs, a, e, slice(0, n))
            at += n


def prepare_rows(x, k_ref, wx, wy, wz, q, start, n, wy_start, ok, z):
    rows = pl.ds(start, n)
    k = k_ref[x, rows, :]
    low, high = k_ref[x, pl.ds(start - 1, n), :], k_ref[x, pl.ds(start + 1, n), :]
    wxl = k + k_ref[x - 1, rows, :]
    ks = jnp.where(z == 0, 0.0, pltpu.roll(k, 1, 1))
    kn = jnp.where(z == NZ - 1, 0.0, pltpu.roll(k, NZ - 1, 1))
    wzl = k + ks
    diagonal = (wxl + (k + k_ref[x + 1, rows, :])) + ((k + low) + (k + high)) + (wzl + (k + kn))
    ok = ok & (diagonal > 0.0)
    q[x, rows, :] = jnp.where(ok, DAMPING / jnp.where(ok, diagonal, 1.0), 0.0)
    wx[x, rows, :] = wxl
    wz[x, rows, :] = jnp.where(z == 0, 0.0, wzl)
    if wy_start is None:
        wy[x, rows, :] = k + low
    else:
        wy[x, pl.ds(wy_start, n), :] = k_ref[x, pl.ds(wy_start, n), :] + k_ref[x, pl.ds(wy_start - 1, n), :]


def neighbours(x, v_ref, wx, wy, wz, start, n, off):
    rows, below, above = pl.ds(start, n), pl.ds(off + (start - 1), n), pl.ds(off + (start + 1), n)
    v = v_ref[x, rows, :]
    wzl = wz[x, rows, :]
    total = wx[x, rows, :] * v_ref[x - 1, rows, :] + wx[x + 1, rows, :] * v_ref[x + 1, rows, :]
    total = total + (wy[x, rows, :] * v_ref[x, below, :] + wy[x, above, :] * v_ref[x, above, :])
    return v, total + (wzl * pltpu.roll(v, 1, 1) + pltpu.roll(wzl * v, NZ - 1, 1))


def sweep_rows(x, old, r2, wx, wy, wz, q, start, n, off):
    v, total = neighbours(x, old, wx, wy, wz, start, n, off)
    rows = pl.ds(start, n)
    return (1.0 - DAMPING) * v + q[x, rows, :] * (r2[x, rows, :] + total)


def residual_rows(x, old, r2, wx, wy, wz, q, start, n, off):
    v, total = neighbours(x, old, wx, wy, wz, start, n, off)
    rows = pl.ds(start, n)
    damped = q[x, rows, :]
    diagonal = DAMPING / jnp.where(damped == 0.0, 1.0, damped)
    return 0.5 * ((r2[x, rows, :] + total) - diagonal * v)


def fill(refs, fields, some, xl, xh):
    for a, dst in enumerate(fields):
        for e in some:
            if a == 2 and e in (0, EX - 1):
                continue
            values = keep(plane_ok(e, xl, xh), halo_plane(refs, a, e, slice(0, CY)))
            dst[e, TOP : TOP + CY, :] = values * 2.0 if a == 2 else values


def inner_steps(ranges, slot, buf, kx, rx, va, vb, vc, wx, wy, wz, q, res, xl, xh):
    off = zero_index()
    z = iota((CY, NZ), 1)
    own = pl.ds(TOP, CY)
    field = (rx, wx, wy, wz, q, TOP, CY, off)

    for lo, hi in ranges[0]:
        for x in range(lo, hi):
            ok = plane_ok(x, xl, xh)
            prepare_rows(x, kx, wx, wy, wz, q, TOP, CY, None, True if ok is None else ok, z)
        wx[hi, own, :] = kx[hi, own, :] + kx[hi - 1, own, :]
    for lo, hi in ranges[0]:
        for x in range(lo, hi):
            vb[x, own, :] = sweep_rows(x, va, *field)
    for lo, hi in ranges[1]:
        for x in range(lo, hi):
            vc[x, own, :] = sweep_rows(x, vb, *field)
    for lo, hi in ranges[2]:
        for x in range(lo, hi):
            at = (x - W) * CY
            res[at : at + CY, :] = residual_rows(x, vc, *field)
            for r in range(at + TOP, at + CY - TOP):
                buf[pl.ds(slot[r], 1), :] = res[r : r + 1, :]


def core_kernel(slot, p_ref, k_ref, r_ref, buf_in, buf, kx, rx, va, vb, vc, wx, wy, wz, q, res, done):
    del buf_in
    fill((p_ref, k_ref, r_ref, None, None, None), (va, kx, rx), range(W, W + CX), None, None)
    a, b = W + 1, W + CX - 1
    ranges = (((a, b),), ((a + 1, b - 1),), ((a + 2, b - 2),))
    inner_steps(ranges, slot, buf, kx, rx, va, vb, vc, wx, wy, wz, q, res, True, True)
    done[...] = jnp.zeros_like(done)


def mid_kernel(slot, from_o, from_e, *refs):
    buf, kx, rx, va, vb, vc, wx, wy, wz, q, res = refs[11:]
    xl, xh, _, _ = edges()
    halo = [*range(W), *range(W + CX, EX)]
    fill((None, None, None, from_o, from_e, is_odd()), (va, kx, rx), halo, xl, xh)
    a, b = W + 1, W + CX - 1
    ranges = tuple(((1 + i, a + i), (b - i, EX - 1 - i)) for i in range(3))
    inner_steps(ranges, slot, buf, kx, rx, va, vb, vc, wx, wy, wz, q, res, xl, xh)


def rim_kernel(
    slot_ref, sl, sh, kx_in, rx_in, va_in, vb_in, vc_in, wx_in, wy_in, wz_in, q_in, res, buf_in,
    kx, rx, va, vb, vc, wx, wy, wz, q, buf, slot, sem,
):
    del kx_in, rx_in, va_in, vb_in, vc_in, wx_in, wy_in, wz_in, q_in, buf_in, res
    table = pltpu.make_async_copy(slot_ref, slot, sem)
    table.start()
    xl, xh, yl, yh = edges()
    off = zero_index()
    end = TOP + CY
    for e in range(1, EX - 1):
        ok = plane_ok(e, xl, xh)
        low_ok, high_ok = (yl, yh) if ok is None else (yl & ok, yh & ok)
        for i, (dst, n, scale) in enumerate(((va, W, 1.0), (kx, W, 1.0), (rx, W - 1, 2.0))):
            at = W * i
            dst[e, TOP - n : TOP, :] = jnp.where(low_ok, sl[e - 1, at : at + n, :], 0.0) * scale
            dst[e, end : end + n, :] = jnp.where(high_ok, sh[e - 1, at : at + n, :], 0.0) * scale
    for e in (0, EX - 1):
        kx[e, TOP - W : TOP, :] = jnp.zeros((W, NZ), F32)
        kx[e, end : end + W, :] = jnp.zeros((W, NZ), F32)
        va[e, TOP - W : TOP, :] = jnp.zeros((W, NZ), F32)
        va[e, end : end + W, :] = jnp.zeros((W, NZ), F32)
    z, y = iota((8, NZ), 1), iota((8, NZ), 0)
    low_rows = (y >= 2) | yl
    high_rows = (y < 6) | yh
    field = (rx, wx, wy, wz, q)
    for x in range(1, EX - 1):
        ok = plane_ok(x, xl, xh)
        ok = True if ok is None else ok
        prepare_rows(x, kx, wx, wy, wz, q, off + (TOP - 2), 8, None, low_rows & ok, z)
        prepare_rows(x, kx, wx, wy, wz, q, off + (end - 6), 8, off + (end - 5), high_rows & ok, z)
    for start in (TOP - 2, end - 6):
        rows = pl.ds(off + start, 8)
        wx[EX - 1, rows, :] = kx[EX - 1, rows, :] + kx[EX - 2, rows, :]
    for x in range(1, EX - 1):
        for start in (TOP - 2, end - 6):
            vb[x, pl.ds(off + start, 8), :] = sweep_rows(x, va, *field, off + start, 8, 0)
    for x in range(2, EX - 2):
        for start in (TOP - 1, end - 7):
            vc[x, pl.ds(off + start, 8), :] = sweep_rows(x, vb, *field, off + start, 8, 0)
    table.wait()
    for x in range(CX):
        for start in (TOP, end - 8):
            out = residual_rows(x + W, vc, *field, start, 8, off)
            for u in range(8):
                buf[pl.ds(slot[x * CY + start - TOP + u], 1), :] = out[u : u + 1]


def parts_of(x):
    a = x.astype(BF16)
    rest = x - a.astype(F32)
    b = rest.astype(BF16)
    return a, b, (rest - b.astype(F32)).astype(BF16)


def coarse_kernel(owners, data, leak_ref, link_ref, back, hot, parts):
    rows = owners * BLOCK
    groups = -(-owners // 3)
    pairs = -(-groups // 2)
    number = (iota((CR, 128), 0) + 1).astype(F32)
    total = jnp.zeros((CR, 3 * NZ), F32)
    bases = []
    for g in range(groups):
        base = g * TRIO
        names = [data[base + t * BLOCK + CAP : base + (t + 1) * BLOCK, :] for t in range(min(3, owners - 3 * g))]
        name = names[0]
        for more in names[1:]:
            name = name + more
        if base + 128 > rows:
            name = pltpu.roll(jnp.broadcast_to(name, (8, 128)), base - (rows - 128), 1)[0:1]
            base = rows - 128
        bases.append(base)
        at = g % 2 * 128
        hot[g // 2, :, at : at + 128] = jnp.where(number == name, 1.0, 0.0).astype(BF16)
        for i, part in enumerate(parts_of(data[base : base + 128, :])):
            parts[g // 2, at : at + 128, i * NZ : (i + 1) * NZ] = part
    if groups % 2:
        hot[pairs - 1, :, 128:] = jnp.zeros((CR, 128), BF16)
        parts[pairs - 1, 128:, :] = jnp.zeros((128, 3 * NZ), BF16)
    for p in range(pairs):
        total = total + jnp.dot(hot[p], parts[p], preferred_element_type=F32)
    total = total[:, 0:NZ] + (total[:, NZ : 2 * NZ] + total[:, 2 * NZ :])

    z = iota((CR, NZ), 1)
    link = link_ref[...]
    inner = jnp.where(z == NZ - 1, 0.0, link)
    below = pltpu.roll(inner, 1, 1)
    w = DAMPING / (leak_ref[...] + link + below)
    u = w * total
    for _ in range(2):
        u = (1.0 - DAMPING) * u + w * (total + inner * pltpu.roll(u, NZ - 1, 1) + pltpu.roll(inner * u, 1, 1))
    pieces = jnp.concatenate(parts_of(u), axis=1)
    for p in range(pairs - 1, -1, -1):
        out = lax.dot_general(hot[p], pieces, (((0,), (0,)), ((), ())), preferred_element_type=F32)
        out = out[:, 0:NZ] + (out[:, NZ : 2 * NZ] + out[:, 2 * NZ :])
        for g in (2 * p + 1, 2 * p):
            if g < groups:
                n = 128 if g == groups - 1 else TRIO
                at = g % 2 * 128
                back[bases[g] : bases[g] + n, :] = out[at : at + n]


EDGE = (0, 1, CX - 2, CX - 1)


def edge_kernel(slot, back, vc, to_o, to_e):
    def fill_planes(low, high):
        for i, x in enumerate(EDGE):
            dst = low if i < 2 else high
            for y in range(CY):
                dst[i % 2, y : y + 1, :] = back[pl.ds(slot[x * CY + y], 1), :] + vc[x + W, TOP + y : TOP + y + 1, :]

    @pl.when(is_odd())
    def _():
        fill_planes(to_e, to_o)

    @pl.when(jnp.logical_not(is_odd()))
    def _():
        fill_planes(to_o, to_e)


def body_kernel(slot, back, vc, to_o, to_e, vd):
    odd = is_odd()
    for i, x in enumerate(EDGE):
        of_o, of_e = to_o[i % 2], to_e[i % 2]
        vd[x + W, TOP : TOP + CY, :] = jnp.where(odd, of_e, of_o) if i < 2 else jnp.where(odd, of_o, of_e)

    def plane(x, carry):
        for y in range(CY):
            row = back[pl.ds(slot[x * CY + y], 1), :] + vc[x + W, TOP + y : TOP + y + 1, :]
            vd[x + W, TOP + y : TOP + y + 1, :] = row
        return carry

    lax.fori_loop(2, CX - 2, plane, 0)


def last_side_kernel(vd, from_o, from_e, to_high, to_low):
    odd = is_odd()
    for dst, rows in ((to_high, slice(CY - 2, CY)), (to_low, slice(0, 2))):
        dst[0] = jnp.where(odd, from_e[1, rows, :], from_o[1, rows, :])
        dst[CX + 1] = jnp.where(odd, from_o[0, rows, :], from_e[0, rows, :])
        for x in range(CX):
            dst[x + 1] = vd[x + W, TOP + rows.start : TOP + rows.stop, :]


def last_inner_kernel(vd_in, from_o, from_e, rx, wx, wy, wz, q, vd, ve, out):
    del vd_in
    xl, xh, _, _ = edges()
    off = zero_index()
    own = pl.ds(TOP, CY)
    odd = is_odd()
    for e in (1, 2):
        of_o, of_e = from_o[e - 1], from_e[e - 1]
        vd[e, own, :] = jnp.where(xl, jnp.where(odd, of_e, of_o), 0.0)
        vd[e + CX + 2, own, :] = jnp.where(xh, jnp.where(odd, of_o, of_e), 0.0)

    field = (rx, wx, wy, wz, q, TOP, CY, off)

    for x in range(2, EX - 2):
        ve[x, own, :] = sweep_rows(x, vd, *field)
    for x in range(CX):
        out[x] = sweep_rows(x + W, ve, *field)


def last_rim_kernel(sl, sh, vd_in, ve_in, inner, rx, wx, wy, wz, q, vd, ve, out):
    del vd_in, ve_in
    xl, xh, yl, yh = edges()
    off = zero_index()
    end = TOP + CY
    for e in range(1, EX - 1):
        if 2 <= e < EX - 2:
            ok = plane_ok(e, xl, xh)
            low_ok, high_ok = (yl, yh) if ok is None else (yl & ok, yh & ok)
            vd[e, TOP - 2 : TOP, :] = jnp.where(low_ok, sl[e - 2], 0.0)
            vd[e, end : end + 2, :] = jnp.where(high_ok, sh[e - 2], 0.0)
        else:
            vd[e, TOP - 2 : TOP, :] = jnp.zeros((2, NZ), F32)
            vd[e, end : end + 2, :] = jnp.zeros((2, NZ), F32)

    field = (rx, wx, wy, wz, q)
    for x in range(2, EX - 2):
        for start in (TOP - 1, end - 7):
            ve[x, pl.ds(off + start, 8), :] = sweep_rows(x, vd, *field, off + start, 8, 0)
    for x in range(CX):
        out[x, 8 : CY - 8, :] = inner[x, 8 : CY - 8, :]
        for start in (TOP, end - 8):
            out[x, start - TOP : start - TOP + 8, :] = sweep_rows(x + W, ve, *field, start, 8, off)


def ring(axis, step):
    n = lax.axis_size(axis)
    return [(i, (i + step) % n) for i in range(n)]


def swap_both(to_o, to_e):
    n = lax.axis_size("bulk")
    got = []
    for first, values in ((1, to_o), (0, to_e)):
        pairs = [(i, (i + 1) % n) for i in range(first, n, 2)]
        got.append(lax.ppermute(values, "bulk", pairs + [(j, i) for i, j in pairs]))
    return got


def from_both(axis, to_high, to_low):
    low = lax.ppermute(to_high, axis, ring(axis, 1))
    high = lax.ppermute(to_low, axis, ring(axis, -1))
    return low, high


EXT = ((EX, EY, NZ), F32)


def cycle(pressure, rhs, kappa, owner, coarse_row, coarse_leak, coarse_link):
    owners = lax.axis_size("bulk")
    slots = owners * BLOCK
    sent = ((2 * W + W - 1, CY, NZ), F32)
    side = ((EX - 2, 8, NZ), F32)
    to_o, to_e = call(
        send_kernel,
        [sent, sent],
        [pltpu.with_memory_space_constraint(f, pltpu.MemorySpace.HBM) for f in (pressure, kappa, rhs)],
        in_specs=[pl.BlockSpec(memory_space=pltpu.MemorySpace.HBM)] * 3,
        scratch=[pltpu.SemaphoreType.DMA((6,))],
        mib=2,
    )
    from_o, from_e = swap_both(to_o, to_e)
    slot, buf = call(
        lambda *refs: slot_kernel(owners, *refs),
        [((8, 128), I32), ((slots, NZ), F32)],
        (owner.reshape(8, 128), coarse_row.reshape(8, 128)),
    )
    table = slot.reshape(CX * CY)
    work = [((slots, NZ), F32)] + [EXT] * 9 + [((CX * CY, NZ), F32)]
    *core, done = call(
        core_kernel,
        work + [((8, NZ), F32)],
        (table, pressure, kappa, rhs, buf),
        in_specs=[SMEM] + [VMEM] * 4,
        aliases={4: 0},
        mib=20,
    )
    to_high, to_low = call(side_kernel, [side, side], (pressure, kappa, rhs, from_o, from_e, done))
    sl, sh = from_both("slab", to_high, to_low)
    buf, *ext, res = call(
        mid_kernel,
        work,
        (table, from_o, from_e, *core),
        in_specs=[SMEM] + [VMEM] * 13,
        aliases={3 + i: i for i in range(11)},
        mib=20,
    )
    *ext, buf = call(
        rim_kernel,
        [EXT] * 9 + [((slots, NZ), F32)],
        (table, sl, sh, *ext, res, buf),
        aliases={**{3 + i: i for i in range(9)}, 13: 9},
        scratch=[pltpu.SMEM((CX * CY,), I32), pltpu.SemaphoreType.DMA],
        mib=20,
    )
    _, rx, _, _, vc, wx, wy, wz, q = ext
    got = lax.all_to_all(buf.reshape(owners, BLOCK, 1, NZ), "bulk", 0, 0)
    (back,) = call(
        lambda *refs: coarse_kernel(owners, *refs),
        [((slots, NZ), F32)],
        (got.reshape(slots, NZ), coarse_leak[0], coarse_link[0]),
        scratch=[pltpu.VMEM((-(-owners // 6), CR, 256), BF16), pltpu.VMEM((-(-owners // 6), 256, 3 * NZ), BF16)],
    )
    back = lax.all_to_all(back.reshape(owners, BLOCK, 1, NZ), "bulk", 0, 0).reshape(slots, NZ)
    to_o, to_e = call(
        edge_kernel, [((2, CY, NZ), F32)] * 2, (table, back, vc), in_specs=[SMEM, VMEM, VMEM]
    )
    from_o, from_e = swap_both(to_o, to_e)
    (vd,) = call(body_kernel, [EXT], (table, back, vc, to_o, to_e), in_specs=[SMEM] + [VMEM] * 4)

    last_side = ((CX + 2, 2, NZ), F32)
    to_high, to_low = call(last_side_kernel, [last_side, last_side], (vd, from_o, from_e))
    sl, sh = from_both("slab", to_high, to_low)
    vd, ve, inner = call(
        last_inner_kernel,
        [EXT, EXT, ((CX, CY, NZ), F32)],
        (vd, from_o, from_e, rx, wx, wy, wz, q),
        aliases={0: 0},
        mib=20,
    )
    _, _, out = call(
        last_rim_kernel,
        [EXT, EXT, ((CX, CY, NZ), F32)],
        (sl, sh, vd, ve, inner, rx, wx, wy, wz, q),
        aliases={2: 0, 3: 1},
        mib=20,
    )
    return out


def solution(mesh):
    return jax.shard_map(
        cycle,
        mesh=mesh,
        in_specs=(
            P("bulk", "slab", None),
            P("bulk", "slab", None),
            P("bulk", "slab", None),
            P("slab", "bulk", None, None),
            P("slab", "bulk", None),
            P("slab", "bulk", None),
            P("slab", "bulk", None),
        ),
        out_specs=P("bulk", "slab", None),
        check_vma=False,
    )
```

```python
import jax
import jax.numpy as jnp
from jax import lax
from jax.experimental import pallas as pl
from jax.experimental.pallas import tpu as pltpu
from jax.sharding import PartitionSpec as P


DAMPING = 0.8
CX, CY, NZ = 16, 64, 128
CR = 128
CAP = 40
BLOCK = CAP + 1
TRIO = 3 * BLOCK
W = 3
TOP = 8
EX, EY = CX + 2 * W, CY + 2 * TOP
F32, BF16, I32 = jnp.float32, jnp.bfloat16, jnp.int32

VMEM = pl.BlockSpec(memory_space=pltpu.VMEM)
SMEM = pl.BlockSpec(memory_space=pltpu.SMEM)


def iota(shape, dim):
    return lax.broadcasted_iota(I32, shape, dim)


def call(kernel, outs, args, in_specs=None, scratch=(), mib=16, aliases=None, out_specs=None):
    return pl.pallas_call(
        kernel,
        out_shape=[jax.ShapeDtypeStruct(s, d) for s, d in outs],
        in_specs=in_specs or [VMEM] * len(args),
        out_specs=out_specs or [VMEM] * len(outs),
        scratch_shapes=list(scratch),
        input_output_aliases=aliases or {},
        compiler_params=pltpu.CompilerParams(vmem_limit_bytes=mib << 20),
    )(*args)


def slot_kernel(owners, own_ref, row_ref, slot_ref, back_ref, buf_ref):
    shift = lax.rem(lax.axis_index("bulk"), 3) * BLOCK
    before = (iota((128, 128), 0) < iota((128, 128), 1)).astype(BF16)
    owner_of = iota((owners, 128), 0)
    lane_of = iota((128, 128), 0)
    seen = jnp.zeros((owners, 1), F32)
    numbers = jnp.zeros((owners, 128), F32)
    for b in range(own_ref.shape[0]):
        own = own_ref[b : b + 1, :]
        mine = owner_of == own
        mine_f = mine.astype(F32)
        count = jnp.dot(mine_f.astype(BF16), before, preferred_element_type=F32) + seen
        rank = jnp.sum(jnp.where(mine, count, 0.0), axis=0, keepdims=True).astype(I32)
        seen = seen + jnp.sum(mine_f, axis=1, keepdims=True)
        slot_ref[b : b + 1, :] = own * BLOCK + rank
        back_ref[b : b + 1, :] = own * CAP + rank
        named = jnp.where(lane_of == rank + shift, (row_ref[b : b + 1, :] + 1).astype(F32), 0.0)
        numbers = numbers + lax.dot_general(
            mine_f.astype(BF16), named.astype(BF16), (((1,), (1,)), ((), ())), preferred_element_type=F32
        )
    buf_ref[...] = jnp.zeros_like(buf_ref)
    for o in range(owners):
        buf_ref[o * BLOCK + CAP : o * BLOCK + BLOCK, :] = numbers[o : o + 1, :]


def edges():
    b, s = lax.axis_index("bulk"), lax.axis_index("slab")
    return b > 0, b < lax.axis_size("bulk") - 1, s > 0, s < lax.axis_size("slab") - 1


def zero_index():
    return jnp.minimum(lax.axis_index("bulk"), 0)


def keep(ok, values):
    return values if ok is None else jnp.where(ok, values, 0.0)


def plane_ok(e, xl, xh):
    return xl if e < W else (None if e < W + CX else xh)


def is_odd():
    return lax.rem(lax.axis_index("bulk"), 2) == 1


def send_kernel(p_ref, k_ref, r_ref, to_o, to_e, sems):
    odd = is_odd()
    copies = []
    at = 0
    for ref, n in ((p_ref, W), (k_ref, W), (r_ref, W - 1)):
        for dst, high in ((to_o, odd), (to_e, jnp.logical_not(odd))):
            src = ref.at[pl.ds(jnp.where(high, CX - n, 0), n)]
            copies.append(pltpu.make_async_copy(src, dst.at[pl.ds(at, n)], sems.at[len(copies)]))
        at += n
    for copy in copies:
        copy.start()
    for copy in copies:
        copy.wait()


def halo_plane(refs, a, e, rows):
    own, from_o, from_e, odd = refs[a], refs[3], refs[4], refs[5]
    if W <= e < W + CX:
        return own[e - W, rows, :]
    low = e < W
    i = W * a + (e - (1 if a == 2 else 0) if low else e - W - CX)
    of_o, of_e = from_o[i, rows, :], from_e[i, rows, :]
    return jnp.where(odd, of_e, of_o) if low else jnp.where(odd, of_o, of_e)


def side_kernel(p_ref, k_ref, r_ref, from_o, from_e, done, to_high, to_low):
    del done
    refs = (p_ref, k_ref, r_ref, from_o, from_e, is_odd())
    for e in range(1, EX - 1):
        at = 0
        for a, n in ((0, W), (1, W), (2, W - 1)):
            to_high[e - 1, at : at + n, :] = halo_plane(refs, a, e, slice(CY - n, CY))
            to_low[e - 1, at : at + n, :] = halo_plane(refs, a, e, slice(0, n))
            at += n


def prepare_rows(x, k_ref, wx, wy, wz, q, start, n, wy_start, ok, z):
    rows = pl.ds(start, n)
    k = k_ref[x, rows, :]
    low, high = k_ref[x, pl.ds(start - 1, n), :], k_ref[x, pl.ds(start + 1, n), :]
    wxl = k + k_ref[x - 1, rows, :]
    ks = jnp.where(z == 0, 0.0, pltpu.roll(k, 1, 1))
    kn = jnp.where(z == NZ - 1, 0.0, pltpu.roll(k, NZ - 1, 1))
    wzl = k + ks
    diagonal = (wxl + (k + k_ref[x + 1, rows, :])) + ((k + low) + (k + high)) + (wzl + (k + kn))
    ok = ok & (diagonal > 0.0)
    q[x, rows, :] = jnp.where(ok, DAMPING / jnp.where(ok, diagonal, 1.0), 0.0)
    wx[x, rows, :] = wxl
    wz[x, rows, :] = jnp.where(z == 0, 0.0, wzl)
    if wy_start is None:
        wy[x, rows, :] = k + low
    else:
        wy[x, pl.ds(wy_start, n), :] = k_ref[x, pl.ds(wy_start, n), :] + k_ref[x, pl.ds(wy_start - 1, n), :]


def neighbours(x, v_ref, wx, wy, wz, start, n, off):
    rows, below, above = pl.ds(start, n), pl.ds(off + (start - 1), n), pl.ds(off + (start + 1), n)
    v = v_ref[x, rows, :]
    wzl = wz[x, rows, :]
    total = wx[x, rows, :] * v_ref[x - 1, rows, :] + wx[x + 1, rows, :] * v_ref[x + 1, rows, :]
    total = total + (wy[x, rows, :] * v_ref[x, below, :] + wy[x, above, :] * v_ref[x, above, :])
    return v, total + (wzl * pltpu.roll(v, 1, 1) + pltpu.roll(wzl * v, NZ - 1, 1))


def sweep_rows(x, old, r2, wx, wy, wz, q, start, n, off):
    v, total = neighbours(x, old, wx, wy, wz, start, n, off)
    rows = pl.ds(start, n)
    return (1.0 - DAMPING) * v + q[x, rows, :] * (r2[x, rows, :] + total)


def residual_rows(x, old, r2, wx, wy, wz, q, start, n, off):
    v, total = neighbours(x, old, wx, wy, wz, start, n, off)
    rows = pl.ds(start, n)
    damped = q[x, rows, :]
    diagonal = DAMPING / jnp.where(damped == 0.0, 1.0, damped)
    return 0.5 * ((r2[x, rows, :] + total) - diagonal * v)


def fill(refs, fields, some, xl, xh):
    for a, dst in enumerate(fields):
        for e in some:
            if a == 2 and e in (0, EX - 1):
                continue
            values = keep(plane_ok(e, xl, xh), halo_plane(refs, a, e, slice(0, CY)))
            dst[e, TOP : TOP + CY, :] = values * 2.0 if a == 2 else values


def inner_steps(ranges, slot, buf, kx, rx, va, vb, vc, wx, wy, wz, q, res, xl, xh):
    off = zero_index()
    z = iota((CY, NZ), 1)
    own = pl.ds(TOP, CY)
    field = (rx, wx, wy, wz, q, TOP, CY, off)

    for lo, hi in ranges[0]:
        for x in range(lo, hi):
            ok = plane_ok(x, xl, xh)
            prepare_rows(x, kx, wx, wy, wz, q, TOP, CY, None, True if ok is None else ok, z)
        wx[hi, own, :] = kx[hi, own, :] + kx[hi - 1, own, :]
    for lo, hi in ranges[0]:
        for x in range(lo, hi):
            vb[x, own, :] = sweep_rows(x, va, *field)
    for lo, hi in ranges[1]:
        for x in range(lo, hi):
            vc[x, own, :] = sweep_rows(x, vb, *field)
    for lo, hi in ranges[2]:
        for x in range(lo, hi):
            at = (x - W) * CY
            res[at : at + CY, :] = residual_rows(x, vc, *field)
            for r in range(at + TOP, at + CY - TOP):
                buf[pl.ds(slot[r], 1), :] = res[r : r + 1, :]


def core_kernel(slot, p_ref, k_ref, r_ref, buf_in, buf, kx, rx, va, vb, vc, wx, wy, wz, q, res, done):
    del buf_in
    fill((p_ref, k_ref, r_ref, None, None, None), (va, kx, rx), range(W, W + CX), None, None)
    a, b = W + 1, W + CX - 1
    ranges = (((a, b),), ((a + 1, b - 1),), ((a + 2, b - 2),))
    inner_steps(ranges, slot, buf, kx, rx, va, vb, vc, wx, wy, wz, q, res, True, True)
    done[...] = jnp.zeros_like(done)


def mid_kernel(slot, from_o, from_e, *refs):
    buf, kx, rx, va, vb, vc, wx, wy, wz, q, res = refs[11:]
    xl, xh, _, _ = edges()
    halo = [*range(W), *range(W + CX, EX)]
    fill((None, None, None, from_o, from_e, is_odd()), (va, kx, rx), halo, xl, xh)
    a, b = W + 1, W + CX - 1
    ranges = tuple(((1 + i, a + i), (b - i, EX - 1 - i)) for i in range(3))
    inner_steps(ranges, slot, buf, kx, rx, va, vb, vc, wx, wy, wz, q, res, xl, xh)


def rim_kernel(
    slot_ref, sl, sh, kx_in, rx_in, va_in, vb_in, vc_in, wx_in, wy_in, wz_in, q_in, res, buf_in,
    kx, rx, va, vb, vc, wx, wy, wz, q, buf, slot, sem,
):
    del kx_in, rx_in, va_in, vb_in, vc_in, wx_in, wy_in, wz_in, q_in, buf_in, res
    table = pltpu.make_async_copy(slot_ref, slot, sem)
    table.start()
    xl, xh, yl, yh = edges()
    off = zero_index()
    end = TOP + CY
    for e in range(1, EX - 1):
        ok = plane_ok(e, xl, xh)
        low_ok, high_ok = (yl, yh) if ok is None else (yl & ok, yh & ok)
        for i, (dst, n, scale) in enumerate(((va, W, 1.0), (kx, W, 1.0), (rx, W - 1, 2.0))):
            at = W * i
            dst[e, TOP - n : TOP, :] = jnp.where(low_ok, sl[e - 1, at : at + n, :], 0.0) * scale
            dst[e, end : end + n, :] = jnp.where(high_ok, sh[e - 1, at : at + n, :], 0.0) * scale
    for e in (0, EX - 1):
        kx[e, TOP - W : TOP, :] = jnp.zeros((W, NZ), F32)
        kx[e, end : end + W, :] = jnp.zeros((W, NZ), F32)
        va[e, TOP - W : TOP, :] = jnp.zeros((W, NZ), F32)
        va[e, end : end + W, :] = jnp.zeros((W, NZ), F32)
    z, y = iota((8, NZ), 1), iota((8, NZ), 0)
    low_rows = (y >= 2) | yl
    high_rows = (y < 6) | yh
    field = (rx, wx, wy, wz, q)
    for x in range(1, EX - 1):
        ok = plane_ok(x, xl, xh)
        ok = True if ok is None else ok
        prepare_rows(x, kx, wx, wy, wz, q, off + (TOP - 2), 8, None, low_rows & ok, z)
        prepare_rows(x, kx, wx, wy, wz, q, off + (end - 6), 8, off + (end - 5), high_rows & ok, z)
    for start in (TOP - 2, end - 6):
        rows = pl.ds(off + start, 8)
        wx[EX - 1, rows, :] = kx[EX - 1, rows, :] + kx[EX - 2, rows, :]
    for x in range(1, EX - 1):
        for start in (TOP - 2, end - 6):
            vb[x, pl.ds(off + start, 8), :] = sweep_rows(x, va, *field, off + start, 8, 0)
    for x in range(2, EX - 2):
        for start in (TOP - 1, end - 7):
            vc[x, pl.ds(off + start, 8), :] = sweep_rows(x, vb, *field, off + start, 8, 0)
    table.wait()
    for x in range(CX):
        for start in (TOP, end - 8):
            out = residual_rows(x + W, vc, *field, start, 8, off)
            for u in range(8):
                buf[pl.ds(slot[x * CY + start - TOP + u], 1), :] = out[u : u + 1]


def parts_of(x):
    a = x.astype(BF16)
    rest = x - a.astype(F32)
    b = rest.astype(BF16)
    return a, b, (rest - b.astype(F32)).astype(BF16)


def coarse_kernel(owners, data, leak_ref, link_ref, back, hot, hot_back, parts):
    rows = owners * BLOCK
    groups = -(-owners // 3)
    pairs = -(-groups // 2)
    number = (iota((CR, 128), 0) + 1).astype(F32)
    total = jnp.zeros((CR, 3 * NZ), F32)
    for g in range(groups):
        base = g * TRIO
        names = [data[base + t * BLOCK + CAP : base + (t + 1) * BLOCK, :] for t in range(min(3, owners - 3 * g))]
        name = name_back = names[0]
        for t, more in enumerate(names[1:], 1):
            name = name + more
            name_back = name_back + pltpu.roll(jnp.broadcast_to(more, (8, 128)), 128 - t, 1)[0:1]
        if base + 128 > rows:
            name = pltpu.roll(jnp.broadcast_to(name, (8, 128)), base - (rows - 128), 1)[0:1]
            base = rows - 128
        at = g % 2 * 128
        hot_back[g // 2, :, at : at + 128] = jnp.where(number == name_back, 1.0, 0.0).astype(BF16)
        hot[g // 2, :, at : at + 128] = jnp.where(number == name, 1.0, 0.0).astype(BF16)
        for i, part in enumerate(parts_of(data[base : base + 128, :])):
            parts[g // 2, at : at + 128, i * NZ : (i + 1) * NZ] = part
    if groups % 2:
        hot[pairs - 1, :, 128:] = jnp.zeros((CR, 128), BF16)
        hot_back[pairs - 1, :, 128:] = jnp.zeros((CR, 128), BF16)
        parts[pairs - 1, 128:, :] = jnp.zeros((128, 3 * NZ), BF16)
    for p in range(pairs):
        total = total + jnp.dot(hot[p], parts[p], preferred_element_type=F32)
    total = total[:, 0:NZ] + (total[:, NZ : 2 * NZ] + total[:, 2 * NZ :])

    z = iota((CR, NZ), 1)
    link = link_ref[...]
    inner = jnp.where(z == NZ - 1, 0.0, link)
    below = pltpu.roll(inner, 1, 1)
    w = DAMPING / (leak_ref[...] + link + below)
    u = w * total
    for _ in range(2):
        u = (1.0 - DAMPING) * u + w * (total + inner * pltpu.roll(u, NZ - 1, 1) + pltpu.roll(inner * u, 1, 1))
    pieces = jnp.concatenate(parts_of(u), axis=1)
    for p in range(pairs):
        out = lax.dot_general(hot_back[p], pieces, (((0,), (0,)), ((), ())), preferred_element_type=F32)
        out = out[:, 0:NZ] + (out[:, NZ : 2 * NZ] + out[:, 2 * NZ :])
        for g in (2 * p, 2 * p + 1):
            if g < groups:
                n = CAP * min(3, owners - 3 * g)
                at = g % 2 * 128
                back[3 * CAP * g : 3 * CAP * g + n, :] = out[at : at + n]


EDGE = (0, 1, CX - 2, CX - 1)


def edge_kernel(slot, back, vc, to_o, to_e):
    def fill_planes(low, high):
        for i, x in enumerate(EDGE):
            dst = low if i < 2 else high
            for y in range(CY):
                dst[i % 2, y : y + 1, :] = back[pl.ds(slot[x * CY + y], 1), :] + vc[x + W, TOP + y : TOP + y + 1, :]

    @pl.when(is_odd())
    def _():
        fill_planes(to_e, to_o)

    @pl.when(jnp.logical_not(is_odd()))
    def _():
        fill_planes(to_o, to_e)


def body_kernel(slot, back, vc, to_o, to_e, vd):
    odd = is_odd()
    for i, x in enumerate(EDGE):
        of_o, of_e = to_o[i % 2], to_e[i % 2]
        vd[x + W, TOP : TOP + CY, :] = jnp.where(odd, of_e, of_o) if i < 2 else jnp.where(odd, of_o, of_e)

    def plane(x, carry):
        for y in range(CY):
            row = back[pl.ds(slot[x * CY + y], 1), :] + vc[x + W, TOP + y : TOP + y + 1, :]
            vd[x + W, TOP + y : TOP + y + 1, :] = row
        return carry

    lax.fori_loop(2, CX - 2, plane, 0)


def last_side_kernel(vd, from_o, from_e, to_high, to_low):
    odd = is_odd()
    for dst, rows in ((to_high, slice(CY - 2, CY)), (to_low, slice(0, 2))):
        dst[0] = jnp.where(odd, from_e[1, rows, :], from_o[1, rows, :])
        dst[CX + 1] = jnp.where(odd, from_o[0, rows, :], from_e[0, rows, :])
        for x in range(CX):
            dst[x + 1] = vd[x + W, TOP + rows.start : TOP + rows.stop, :]


def last_inner_kernel(vd_in, from_o, from_e, rx, wx, wy, wz, q, vd, ve, out):
    del vd_in
    xl, xh, _, _ = edges()
    off = zero_index()
    own = pl.ds(TOP, CY)
    odd = is_odd()
    for e in (1, 2):
        of_o, of_e = from_o[e - 1], from_e[e - 1]
        vd[e, own, :] = jnp.where(xl, jnp.where(odd, of_e, of_o), 0.0)
        vd[e + CX + 2, own, :] = jnp.where(xh, jnp.where(odd, of_o, of_e), 0.0)

    field = (rx, wx, wy, wz, q, TOP, CY, off)

    for x in range(2, EX - 2):
        ve[x, own, :] = sweep_rows(x, vd, *field)
    for x in range(CX):
        out[x] = sweep_rows(x + W, ve, *field)


def last_rim_kernel(sl, sh, vd_in, ve_in, inner, rx, wx, wy, wz, q, vd, ve, out):
    del vd_in, ve_in
    xl, xh, yl, yh = edges()
    off = zero_index()
    end = TOP + CY
    for e in range(1, EX - 1):
        if 2 <= e < EX - 2:
            ok = plane_ok(e, xl, xh)
            low_ok, high_ok = (yl, yh) if ok is None else (yl & ok, yh & ok)
            vd[e, TOP - 2 : TOP, :] = jnp.where(low_ok, sl[e - 2], 0.0)
            vd[e, end : end + 2, :] = jnp.where(high_ok, sh[e - 2], 0.0)
        else:
            vd[e, TOP - 2 : TOP, :] = jnp.zeros((2, NZ), F32)
            vd[e, end : end + 2, :] = jnp.zeros((2, NZ), F32)

    field = (rx, wx, wy, wz, q)
    for x in range(2, EX - 2):
        for start in (TOP - 1, end - 7):
            ve[x, pl.ds(off + start, 8), :] = sweep_rows(x, vd, *field, off + start, 8, 0)
    for x in range(CX):
        out[x, 8 : CY - 8, :] = inner[x, 8 : CY - 8, :]
        for start in (TOP, end - 8):
            out[x, start - TOP : start - TOP + 8, :] = sweep_rows(x + W, ve, *field, start, 8, off)


def ring(axis, step):
    n = lax.axis_size(axis)
    return [(i, (i + step) % n) for i in range(n)]


def swap_both(to_o, to_e):
    n = lax.axis_size("bulk")
    got = []
    for first, values in ((1, to_o), (0, to_e)):
        pairs = [(i, i + 1) for i in range(first, n - 1, 2)]
        alone = [(i, i) for i in (0, n - 1)] if first else []
        got.append(lax.ppermute(values, "bulk", pairs + [(j, i) for i, j in pairs] + alone))
    return got


def from_both(axis, to_high, to_low):
    low = lax.ppermute(to_high, axis, ring(axis, 1))
    high = lax.ppermute(to_low, axis, ring(axis, -1))
    return low, high


EXT = ((EX, EY, NZ), F32)


def cycle(pressure, rhs, kappa, owner, coarse_row, coarse_leak, coarse_link):
    owners = lax.axis_size("bulk")
    slots = owners * BLOCK
    sent = ((2 * W + W - 1, CY, NZ), F32)
    side = ((EX - 2, 8, NZ), F32)
    to_o, to_e = call(
        send_kernel,
        [sent, sent],
        [pltpu.with_memory_space_constraint(f, pltpu.MemorySpace.HBM) for f in (pressure, kappa, rhs)],
        in_specs=[pl.BlockSpec(memory_space=pltpu.MemorySpace.HBM)] * 3,
        scratch=[pltpu.SemaphoreType.DMA((6,))],
        mib=2,
    )
    from_o, from_e = swap_both(to_o, to_e)
    slot, slot_back, buf = call(
        lambda *refs: slot_kernel(owners, *refs),
        [((8, 128), I32), ((8, 128), I32), ((slots, NZ), F32)],
        (owner.reshape(8, 128), coarse_row.reshape(8, 128)),
    )
    table, table_back = slot.reshape(CX * CY), slot_back.reshape(CX * CY)
    work = [((slots, NZ), F32)] + [EXT] * 9 + [((CX * CY, NZ), F32)]
    *core, done = call(
        core_kernel,
        work + [((8, NZ), F32)],
        (table, pressure, kappa, rhs, buf),
        in_specs=[SMEM] + [VMEM] * 4,
        aliases={4: 0},
        mib=20,
    )
    to_high, to_low = call(side_kernel, [side, side], (pressure, kappa, rhs, from_o, from_e, done))
    sl, sh = from_both("slab", to_high, to_low)
    buf, *ext, res = call(
        mid_kernel,
        work,
        (table, from_o, from_e, *core),
        in_specs=[SMEM] + [VMEM] * 13,
        aliases={3 + i: i for i in range(11)},
        mib=20,
    )
    *ext, buf = call(
        rim_kernel,
        [EXT] * 9 + [((slots, NZ), F32)],
        (table, sl, sh, *ext, res, buf),
        aliases={**{3 + i: i for i in range(9)}, 13: 9},
        scratch=[pltpu.SMEM((CX * CY,), I32), pltpu.SemaphoreType.DMA],
        mib=20,
    )
    _, rx, _, _, vc, wx, wy, wz, q = ext
    got = lax.all_to_all(buf.reshape(owners, BLOCK, 1, NZ), "bulk", 0, 0)
    (back,) = call(
        lambda *refs: coarse_kernel(owners, *refs),
        [((owners * CAP, NZ), F32)],
        (got.reshape(slots, NZ), coarse_leak[0], coarse_link[0]),
        scratch=[pltpu.VMEM((-(-owners // 6), CR, 256), BF16), pltpu.VMEM((-(-owners // 6), CR, 256), BF16), pltpu.VMEM((-(-owners // 6), 256, 3 * NZ), BF16)],
    )
    back = lax.all_to_all(back.reshape(owners, CAP, 1, NZ), "bulk", 0, 0).reshape(owners * CAP, NZ)
    to_o, to_e = call(
        edge_kernel, [((2, CY, NZ), F32)] * 2, (table_back, back, vc), in_specs=[SMEM, VMEM, VMEM]
    )
    from_o, from_e = swap_both(to_o, to_e)
    (vd,) = call(body_kernel, [EXT], (table_back, back, vc, to_o, to_e), in_specs=[SMEM] + [VMEM] * 4)

    last_side = ((CX + 2, 2, NZ), F32)
    to_high, to_low = call(last_side_kernel, [last_side, last_side], (vd, from_o, from_e))
    sl, sh = from_both("slab", to_high, to_low)
    vd, ve, inner = call(
        last_inner_kernel,
        [EXT, EXT, ((CX, CY, NZ), F32)],
        (vd, from_o, from_e, rx, wx, wy, wz, q),
        aliases={0: 0},
        mib=20,
    )
    _, _, out = call(
        last_rim_kernel,
        [EXT, EXT, ((CX, CY, NZ), F32)],
        (sl, sh, vd, ve, inner, rx, wx, wy, wz, q),
        aliases={2: 0, 3: 1},
        mib=20,
    )
    return out


def solution(mesh):
    return jax.shard_map(
        cycle,
        mesh=mesh,
        in_specs=(
            P("bulk", "slab", None),
            P("bulk", "slab", None),
            P("bulk", "slab", None),
            P("slab", "bulk", None, None),
            P("slab", "bulk", None),
            P("slab", "bulk", None),
            P("slab", "bulk", None),
        ),
        out_specs=P("bulk", "slab", None),
        check_vma=False,
    )
```

```python
import jax
import jax.numpy as jnp
from jax import lax
from jax.experimental import pallas as pl
from jax.experimental.pallas import tpu as pltpu
from jax.sharding import PartitionSpec as P


DAMPING = 0.8
CX, CY, NZ = 16, 64, 128
CR = 128
CAP = 40
BLOCK = CAP + 1
TRIO = 3 * BLOCK
W = 3
TOP = 8
EX, EY = CX + 2 * W, CY + 2 * TOP
F32, BF16, I32 = jnp.float32, jnp.bfloat16, jnp.int32

VMEM = pl.BlockSpec(memory_space=pltpu.VMEM)
SMEM = pl.BlockSpec(memory_space=pltpu.SMEM)


def iota(shape, dim):
    return lax.broadcasted_iota(I32, shape, dim)


def call(kernel, outs, args, in_specs=None, scratch=(), mib=16, aliases=None, out_specs=None):
    return pl.pallas_call(
        kernel,
        out_shape=[jax.ShapeDtypeStruct(s, d) for s, d in outs],
        in_specs=in_specs or [VMEM] * len(args),
        out_specs=out_specs or [VMEM] * len(outs),
        scratch_shapes=list(scratch),
        input_output_aliases=aliases or {},
        compiler_params=pltpu.CompilerParams(vmem_limit_bytes=mib << 20),
    )(*args)


def slot_kernel(owners, own_ref, row_ref, slot_ref, back_ref, buf_ref):
    shift = lax.rem(lax.axis_index("bulk"), 3) * BLOCK
    before = (iota((128, 128), 0) < iota((128, 128), 1)).astype(BF16)
    owner_of = iota((owners, 128), 0)
    lane_of = iota((128, 128), 0)
    seen = jnp.zeros((owners, 1), F32)
    numbers = jnp.zeros((owners, 128), F32)
    for b in range(own_ref.shape[0]):
        own = own_ref[b : b + 1, :]
        mine = owner_of == own
        mine_f = mine.astype(F32)
        count = jnp.dot(mine_f.astype(BF16), before, preferred_element_type=F32) + seen
        rank = jnp.sum(jnp.where(mine, count, 0.0), axis=0, keepdims=True).astype(I32)
        seen = seen + jnp.sum(mine_f, axis=1, keepdims=True)
        slot_ref[b : b + 1, :] = own * BLOCK + rank
        back_ref[b : b + 1, :] = own * CAP + rank
        named = jnp.where(lane_of == rank + shift, (row_ref[b : b + 1, :] + 1).astype(F32), 0.0)
        numbers = numbers + lax.dot_general(
            mine_f.astype(BF16), named.astype(BF16), (((1,), (1,)), ((), ())), preferred_element_type=F32
        )
    buf_ref[...] = jnp.zeros_like(buf_ref)
    for o in range(owners):
        buf_ref[o * BLOCK + CAP : o * BLOCK + BLOCK, :] = numbers[o : o + 1, :]


def edges():
    b, s = lax.axis_index("bulk"), lax.axis_index("slab")
    return b > 0, b < lax.axis_size("bulk") - 1, s > 0, s < lax.axis_size("slab") - 1


def zero_index():
    return jnp.minimum(lax.axis_index("bulk"), 0)


def keep(ok, values):
    return values if ok is None else jnp.where(ok, values, 0.0)


def plane_ok(e, xl, xh):
    return xl if e < W else (None if e < W + CX else xh)


def is_odd():
    return lax.rem(lax.axis_index("bulk"), 2) == 1


def send_kernel(p_ref, k_ref, r_ref, to_o, to_e, sems):
    odd = is_odd()
    copies = []
    at = 0
    for ref, n in ((p_ref, W), (k_ref, W), (r_ref, W - 1)):
        for dst, high in ((to_o, odd), (to_e, jnp.logical_not(odd))):
            src = ref.at[pl.ds(jnp.where(high, CX - n, 0), n)]
            copies.append(pltpu.make_async_copy(src, dst.at[pl.ds(at, n)], sems.at[len(copies)]))
        at += n
    for copy in copies:
        copy.start()
    for copy in copies:
        copy.wait()


def halo_plane(refs, a, e, rows):
    own, from_o, from_e, odd = refs[a], refs[3], refs[4], refs[5]
    if W <= e < W + CX:
        return own[e - W, rows, :]
    low = e < W
    i = W * a + (e - (1 if a == 2 else 0) if low else e - W - CX)
    of_o, of_e = from_o[i, rows, :], from_e[i, rows, :]
    return jnp.where(odd, of_e, of_o) if low else jnp.where(odd, of_o, of_e)


def side_kernel(p_ref, k_ref, r_ref, from_o, from_e, done, to_high, to_low):
    del done
    refs = (p_ref, k_ref, r_ref, from_o, from_e, is_odd())
    for e in range(1, EX - 1):
        at = 0
        for a, n in ((0, W), (1, W), (2, W - 1)):
            to_high[e - 1, at : at + n, :] = halo_plane(refs, a, e, slice(CY - n, CY))
            to_low[e - 1, at : at + n, :] = halo_plane(refs, a, e, slice(0, n))
            at += n


def prepare_rows(x, k_ref, wx, wy, wz, q, start, n, wy_start, ok, z):
    rows = pl.ds(start, n)
    k = k_ref[x, rows, :]
    low, high = k_ref[x, pl.ds(start - 1, n), :], k_ref[x, pl.ds(start + 1, n), :]
    wxl = k + k_ref[x - 1, rows, :]
    ks = jnp.where(z == 0, 0.0, pltpu.roll(k, 1, 1))
    kn = jnp.where(z == NZ - 1, 0.0, pltpu.roll(k, NZ - 1, 1))
    wzl = k + ks
    diagonal = (wxl + (k + k_ref[x + 1, rows, :])) + ((k + low) + (k + high)) + (wzl + (k + kn))
    ok = ok & (diagonal > 0.0)
    q[x, rows, :] = jnp.where(ok, DAMPING / jnp.where(ok, diagonal, 1.0), 0.0)
    wx[x, rows, :] = wxl
    wz[x, rows, :] = jnp.where(z == 0, 0.0, wzl)
    if wy_start is None:
        wy[x, rows, :] = k + low
    else:
        wy[x, pl.ds(wy_start, n), :] = k_ref[x, pl.ds(wy_start, n), :] + k_ref[x, pl.ds(wy_start - 1, n), :]


def neighbours(x, v_ref, wx, wy, wz, start, n, off):
    rows, below, above = pl.ds(start, n), pl.ds(off + (start - 1), n), pl.ds(off + (start + 1), n)
    v = v_ref[x, rows, :]
    wzl = wz[x, rows, :]
    total = wx[x, rows, :] * v_ref[x - 1, rows, :] + wx[x + 1, rows, :] * v_ref[x + 1, rows, :]
    total = total + (wy[x, rows, :] * v_ref[x, below, :] + wy[x, above, :] * v_ref[x, above, :])
    return v, total + (wzl * pltpu.roll(v, 1, 1) + pltpu.roll(wzl * v, NZ - 1, 1))


def sweep_rows(x, old, r2, wx, wy, wz, q, start, n, off):
    v, total = neighbours(x, old, wx, wy, wz, start, n, off)
    rows = pl.ds(start, n)
    return (1.0 - DAMPING) * v + q[x, rows, :] * (r2[x, rows, :] + total)


def residual_rows(x, old, r2, wx, wy, wz, q, start, n, off):
    v, total = neighbours(x, old, wx, wy, wz, start, n, off)
    rows = pl.ds(start, n)
    damped = q[x, rows, :]
    diagonal = DAMPING / jnp.where(damped == 0.0, 1.0, damped)
    return 0.5 * ((r2[x, rows, :] + total) - diagonal * v)


def fill(refs, fields, some, xl, xh):
    for a, dst in enumerate(fields):
        for e in some:
            if a == 2 and e in (0, EX - 1):
                continue
            values = keep(plane_ok(e, xl, xh), halo_plane(refs, a, e, slice(0, CY)))
            dst[e, TOP : TOP + CY, :] = values * 2.0 if a == 2 else values


def inner_steps(ranges, slot, buf, kx, rx, va, vb, vc, wx, wy, wz, q, res, xl, xh):
    off = zero_index()
    z = iota((CY, NZ), 1)
    own = pl.ds(TOP, CY)
    field = (rx, wx, wy, wz, q, TOP, CY, off)

    for lo, hi in ranges[0]:
        for x in range(lo, hi):
            ok = plane_ok(x, xl, xh)
            prepare_rows(x, kx, wx, wy, wz, q, TOP, CY, None, True if ok is None else ok, z)
        wx[hi, own, :] = kx[hi, own, :] + kx[hi - 1, own, :]
    for lo, hi in ranges[0]:
        for x in range(lo, hi):
            vb[x, own, :] = sweep_rows(x, va, *field)
    for lo, hi in ranges[1]:
        for x in range(lo, hi):
            vc[x, own, :] = sweep_rows(x, vb, *field)
    for lo, hi in ranges[2]:
        for x in range(lo, hi):
            at = (x - W) * CY
            res[at : at + CY, :] = residual_rows(x, vc, *field)
            for r in range(at + TOP, at + CY - TOP):
                buf[pl.ds(slot[r], 1), :] = res[r : r + 1, :]


def core_kernel(slot, p_ref, k_ref, r_ref, buf_in, buf, kx, rx, va, vb, vc, wx, wy, wz, q, res, done):
    del buf_in
    fill((p_ref, k_ref, r_ref, None, None, None), (va, kx, rx), range(W, W + CX), None, None)
    a, b = W + 1, W + CX - 1
    ranges = (((a, b),), ((a + 1, b - 1),), ((a + 2, b - 2),))
    inner_steps(ranges, slot, buf, kx, rx, va, vb, vc, wx, wy, wz, q, res, True, True)
    done[...] = jnp.zeros_like(done)


def mid_kernel(slot, from_o, from_e, *refs):
    buf, kx, rx, va, vb, vc, wx, wy, wz, q, res = refs[11:]
    xl, xh, _, _ = edges()
    halo = [*range(W), *range(W + CX, EX)]
    fill((None, None, None, from_o, from_e, is_odd()), (va, kx, rx), halo, xl, xh)
    a, b = W + 1, W + CX - 1
    ranges = tuple(((1 + i, a + i), (b - i, EX - 1 - i)) for i in range(3))
    inner_steps(ranges, slot, buf, kx, rx, va, vb, vc, wx, wy, wz, q, res, xl, xh)


def rim_kernel(
    slot_ref, sl, sh, kx_in, rx_in, va_in, vb_in, vc_in, wx_in, wy_in, wz_in, q_in, res, buf_in,
    kx, rx, va, vb, vc, wx, wy, wz, q, buf, slot, sem,
):
    del kx_in, rx_in, va_in, vb_in, vc_in, wx_in, wy_in, wz_in, q_in, buf_in, res
    table = pltpu.make_async_copy(slot_ref, slot, sem)
    table.start()
    xl, xh, yl, yh = edges()
    off = zero_index()
    end = TOP + CY
    for e in range(1, EX - 1):
        ok = plane_ok(e, xl, xh)
        low_ok, high_ok = (yl, yh) if ok is None else (yl & ok, yh & ok)
        for i, (dst, n, scale) in enumerate(((va, W, 1.0), (kx, W, 1.0), (rx, W - 1, 2.0))):
            at = W * i
            dst[e, TOP - n : TOP, :] = jnp.where(low_ok, sl[e - 1, at : at + n, :], 0.0) * scale
            dst[e, end : end + n, :] = jnp.where(high_ok, sh[e - 1, at : at + n, :], 0.0) * scale
    for e in (0, EX - 1):
        kx[e, TOP - W : TOP, :] = jnp.zeros((W, NZ), F32)
        kx[e, end : end + W, :] = jnp.zeros((W, NZ), F32)
        va[e, TOP - W : TOP, :] = jnp.zeros((W, NZ), F32)
        va[e, end : end + W, :] = jnp.zeros((W, NZ), F32)
    z, y = iota((8, NZ), 1), iota((8, NZ), 0)
    low_rows = (y >= 2) | yl
    high_rows = (y < 6) | yh
    field = (rx, wx, wy, wz, q)
    for x in range(1, EX - 1):
        ok = plane_ok(x, xl, xh)
        ok = True if ok is None else ok
        prepare_rows(x, kx, wx, wy, wz, q, off + (TOP - 2), 8, None, low_rows & ok, z)
        prepare_rows(x, kx, wx, wy, wz, q, off + (end - 6), 8, off + (end - 5), high_rows & ok, z)
    for start in (TOP - 2, end - 6):
        rows = pl.ds(off + start, 8)
        wx[EX - 1, rows, :] = kx[EX - 1, rows, :] + kx[EX - 2, rows, :]
    for x in range(1, EX - 1):
        for start in (TOP - 2, end - 6):
            vb[x, pl.ds(off + start, 8), :] = sweep_rows(x, va, *field, off + start, 8, 0)
    for x in range(2, EX - 2):
        for start in (TOP - 1, end - 7):
            vc[x, pl.ds(off + start, 8), :] = sweep_rows(x, vb, *field, off + start, 8, 0)
    table.wait()
    for x in range(CX):
        for start in (TOP, end - 8):
            out = residual_rows(x + W, vc, *field, start, 8, off)
            for u in range(8):
                buf[pl.ds(slot[x * CY + start - TOP + u], 1), :] = out[u : u + 1]


def parts_of(x):
    a = x.astype(BF16)
    rest = x - a.astype(F32)
    b = rest.astype(BF16)
    return a, b, (rest - b.astype(F32)).astype(BF16)


def coarse_kernel(owners, data, leak_ref, link_ref, back, hot, hot_back, parts):
    rows = owners * BLOCK
    groups = -(-owners // 3)
    pairs = -(-groups // 2)
    number = (iota((CR, 128), 0) + 1).astype(F32)
    total = jnp.zeros((CR, 3 * NZ), F32)
    for g in range(groups):
        base = g * TRIO
        names = [data[base + t * BLOCK + CAP : base + (t + 1) * BLOCK, :] for t in range(min(3, owners - 3 * g))]
        name = name_back = names[0]
        for t, more in enumerate(names[1:], 1):
            name = name + more
            name_back = name_back + pltpu.roll(jnp.broadcast_to(more, (8, 128)), 128 - t, 1)[0:1]
        if base + 128 > rows:
            name = pltpu.roll(jnp.broadcast_to(name, (8, 128)), base - (rows - 128), 1)[0:1]
            base = rows - 128
        at = g % 2 * 128
        hot_back[g // 2, :, at : at + 128] = jnp.where(number == name_back, 1.0, 0.0).astype(BF16)
        hot[g // 2, :, at : at + 128] = jnp.where(number == name, 1.0, 0.0).astype(BF16)
        for i, part in enumerate(parts_of(data[base : base + 128, :])):
            parts[g // 2, at : at + 128, i * NZ : (i + 1) * NZ] = part
    if groups % 2:
        hot[pairs - 1, :, 128:] = jnp.zeros((CR, 128), BF16)
        hot_back[pairs - 1, :, 128:] = jnp.zeros((CR, 128), BF16)
        parts[pairs - 1, 128:, :] = jnp.zeros((128, 3 * NZ), BF16)
    for p in range(pairs):
        total = total + jnp.dot(hot[p], parts[p], preferred_element_type=F32)
    total = total[:, 0:NZ] + (total[:, NZ : 2 * NZ] + total[:, 2 * NZ :])

    z = iota((CR, NZ), 1)
    link = link_ref[...]
    inner = jnp.where(z == NZ - 1, 0.0, link)
    below = pltpu.roll(inner, 1, 1)
    w = DAMPING / (leak_ref[...] + link + below)
    u = w * total
    for _ in range(2):
        u = (1.0 - DAMPING) * u + w * (total + inner * pltpu.roll(u, NZ - 1, 1) + pltpu.roll(inner * u, 1, 1))
    pieces = jnp.concatenate(parts_of(u), axis=1)
    for p in range(pairs):
        out = lax.dot_general(hot_back[p], pieces, (((0,), (0,)), ((), ())), preferred_element_type=F32)
        out = out[:, 0:NZ] + (out[:, NZ : 2 * NZ] + out[:, 2 * NZ :])
        for g in (2 * p, 2 * p + 1):
            if g < groups:
                n = CAP * min(3, owners - 3 * g)
                at = g % 2 * 128
                back[3 * CAP * g : 3 * CAP * g + n, :] = out[at : at + n]


EDGE = (0, 1, CX - 2, CX - 1)


def edge_kernel(slot, back, vc, to_o, to_e):
    def fill_planes(low, high):
        for i, x in enumerate(EDGE):
            dst = low if i < 2 else high
            for y in range(CY):
                dst[i % 2, y : y + 1, :] = back[pl.ds(slot[x * CY + y], 1), :] + vc[x + W, TOP + y : TOP + y + 1, :]

    @pl.when(is_odd())
    def _():
        fill_planes(to_e, to_o)

    @pl.when(jnp.logical_not(is_odd()))
    def _():
        fill_planes(to_o, to_e)


def body_kernel(slot, back, vc, to_o, to_e, vd):
    odd = is_odd()
    for i, x in enumerate(EDGE):
        of_o, of_e = to_o[i % 2], to_e[i % 2]
        vd[x + W, TOP : TOP + CY, :] = jnp.where(odd, of_e, of_o) if i < 2 else jnp.where(odd, of_o, of_e)

    def plane(x, carry):
        for y in range(CY):
            row = back[pl.ds(slot[x * CY + y], 1), :] + vc[x + W, TOP + y : TOP + y + 1, :]
            vd[x + W, TOP + y : TOP + y + 1, :] = row
        return carry

    lax.fori_loop(2, CX - 2, plane, 0)


def last_side_kernel(vd, from_o, from_e, to_high, to_low):
    odd = is_odd()
    for dst, rows in ((to_high, slice(CY - 2, CY)), (to_low, slice(0, 2))):
        dst[0] = jnp.where(odd, from_e[1, rows, :], from_o[1, rows, :])
        dst[CX + 1] = jnp.where(odd, from_o[0, rows, :], from_e[0, rows, :])
        for x in range(CX):
            dst[x + 1] = vd[x + W, TOP + rows.start : TOP + rows.stop, :]


def last_inner_kernel(vd_in, from_o, from_e, rx, wx, wy, wz, q, vd, ve, out):
    del vd_in
    xl, xh, _, _ = edges()
    off = zero_index()
    own = pl.ds(TOP, CY)
    odd = is_odd()
    for e in (1, 2):
        of_o, of_e = from_o[e - 1], from_e[e - 1]
        vd[e, own, :] = jnp.where(xl, jnp.where(odd, of_e, of_o), 0.0)
        vd[e + CX + 2, own, :] = jnp.where(xh, jnp.where(odd, of_o, of_e), 0.0)

    field = (rx, wx, wy, wz, q, TOP, CY, off)

    for x in range(2, EX - 2):
        ve[x, own, :] = sweep_rows(x, vd, *field)
    for x in range(CX):
        out[x] = sweep_rows(x + W, ve, *field)


def last_rim_kernel(sl, sh, vd_in, ve_in, inner, rx, wx, wy, wz, q, vd, ve, out):
    del vd_in, ve_in
    xl, xh, yl, yh = edges()
    off = zero_index()
    end = TOP + CY
    for e in range(1, EX - 1):
        if 2 <= e < EX - 2:
            ok = plane_ok(e, xl, xh)
            low_ok, high_ok = (yl, yh) if ok is None else (yl & ok, yh & ok)
            vd[e, TOP - 2 : TOP, :] = jnp.where(low_ok, sl[e - 2], 0.0)
            vd[e, end : end + 2, :] = jnp.where(high_ok, sh[e - 2], 0.0)
        else:
            vd[e, TOP - 2 : TOP, :] = jnp.zeros((2, NZ), F32)
            vd[e, end : end + 2, :] = jnp.zeros((2, NZ), F32)

    field = (rx, wx, wy, wz, q)
    for x in range(2, EX - 2):
        for start in (TOP - 1, end - 7):
            ve[x, pl.ds(off + start, 8), :] = sweep_rows(x, vd, *field, off + start, 8, 0)
    for x in range(CX):
        out[x, 8 : CY - 8, :] = inner[x, 8 : CY - 8, :]
        for start in (TOP, end - 8):
            out[x, start - TOP : start - TOP + 8, :] = sweep_rows(x + W, ve, *field, start, 8, off)


def ring(axis, step):
    n = lax.axis_size(axis)
    return [(i, (i + step) % n) for i in range(n)]


def swap_both(to_o, to_e):
    n, m = lax.axis_size("bulk"), lax.axis_size("slab")
    got = []
    for first, values in ((1, to_o), (0, to_e)):
        pairs = [(i * m + s, (i + 1) * m + s) for i in range(first, n - 1, 2) for s in range(m)]
        if first:
            pairs += [(i * m + s, i * m + s + 1) for i in (0, n - 1) for s in range(0, m, 2)]
        got.append(lax.ppermute(values, ("bulk", "slab"), pairs + [(j, i) for i, j in pairs]))
    return got


def from_both(axis, to_high, to_low):
    low = lax.ppermute(to_high, axis, ring(axis, 1))
    high = lax.ppermute(to_low, axis, ring(axis, -1))
    return low, high


EXT = ((EX, EY, NZ), F32)


def cycle(pressure, rhs, kappa, owner, coarse_row, coarse_leak, coarse_link):
    owners = lax.axis_size("bulk")
    slots = owners * BLOCK
    sent = ((2 * W + W - 1, CY, NZ), F32)
    side = ((EX - 2, 8, NZ), F32)
    to_o, to_e = call(
        send_kernel,
        [sent, sent],
        [pltpu.with_memory_space_constraint(f, pltpu.MemorySpace.HBM) for f in (pressure, kappa, rhs)],
        in_specs=[pl.BlockSpec(memory_space=pltpu.MemorySpace.HBM)] * 3,
        scratch=[pltpu.SemaphoreType.DMA((6,))],
        mib=2,
    )
    from_o, from_e = swap_both(to_o, to_e)
    slot, slot_back, buf = call(
        lambda *refs: slot_kernel(owners, *refs),
        [((8, 128), I32), ((8, 128), I32), ((slots, NZ), F32)],
        (owner.reshape(8, 128), coarse_row.reshape(8, 128)),
    )
    table, table_back = slot.reshape(CX * CY), slot_back.reshape(CX * CY)
    work = [((slots, NZ), F32)] + [EXT] * 9 + [((CX * CY, NZ), F32)]
    *core, done = call(
        core_kernel,
        work + [((8, NZ), F32)],
        (table, pressure, kappa, rhs, buf),
        in_specs=[SMEM] + [VMEM] * 4,
        aliases={4: 0},
        mib=20,
    )
    to_high, to_low = call(side_kernel, [side, side], (pressure, kappa, rhs, from_o, from_e, done))
    sl, sh = from_both("slab", to_high, to_low)
    buf, *ext, res = call(
        mid_kernel,
        work,
        (table, from_o, from_e, *core),
        in_specs=[SMEM] + [VMEM] * 13,
        aliases={3 + i: i for i in range(11)},
        mib=20,
    )
    *ext, buf = call(
        rim_kernel,
        [EXT] * 9 + [((slots, NZ), F32)],
        (table, sl, sh, *ext, res, buf),
        aliases={**{3 + i: i for i in range(9)}, 13: 9},
        scratch=[pltpu.SMEM((CX * CY,), I32), pltpu.SemaphoreType.DMA],
        mib=20,
    )
    _, rx, _, _, vc, wx, wy, wz, q = ext
    got = lax.all_to_all(buf.reshape(owners, BLOCK, 1, NZ), "bulk", 0, 0)
    (back,) = call(
        lambda *refs: coarse_kernel(owners, *refs),
        [((owners * CAP, NZ), F32)],
        (got.reshape(slots, NZ), coarse_leak[0], coarse_link[0]),
        scratch=[pltpu.VMEM((-(-owners // 6), CR, 256), BF16), pltpu.VMEM((-(-owners // 6), CR, 256), BF16), pltpu.VMEM((-(-owners // 6), 256, 3 * NZ), BF16)],
    )
    back = lax.all_to_all(back.reshape(owners, CAP, 1, NZ), "bulk", 0, 0).reshape(owners * CAP, NZ)
    to_o, to_e = call(
        edge_kernel, [((2, CY, NZ), F32)] * 2, (table_back, back, vc), in_specs=[SMEM, VMEM, VMEM]
    )
    from_o, from_e = swap_both(to_o, to_e)
    (vd,) = call(body_kernel, [EXT], (table_back, back, vc, to_o, to_e), in_specs=[SMEM] + [VMEM] * 4)

    last_side = ((CX + 2, 2, NZ), F32)
    to_high, to_low = call(last_side_kernel, [last_side, last_side], (vd, from_o, from_e))
    sl, sh = from_both("slab", to_high, to_low)
    vd, ve, inner = call(
        last_inner_kernel,
        [EXT, EXT, ((CX, CY, NZ), F32)],
        (vd, from_o, from_e, rx, wx, wy, wz, q),
        aliases={0: 0},
        mib=20,
    )
    _, _, out = call(
        last_rim_kernel,
        [EXT, EXT, ((CX, CY, NZ), F32)],
        (sl, sh, vd, ve, inner, rx, wx, wy, wz, q),
        aliases={2: 0, 3: 1},
        mib=20,
    )
    return out


def solution(mesh):
    return jax.shard_map(
        cycle,
        mesh=mesh,
        in_specs=(
            P("bulk", "slab", None),
            P("bulk", "slab", None),
            P("bulk", "slab", None),
            P("slab", "bulk", None, None),
            P("slab", "bulk", None),
            P("slab", "bulk", None),
            P("slab", "bulk", None),
        ),
        out_specs=P("bulk", "slab", None),
        check_vma=False,
    )
```

```python
import jax
import jax.numpy as jnp
from jax import lax
from jax.experimental import pallas as pl
from jax.experimental.pallas import tpu as pltpu
from jax.sharding import PartitionSpec as P


DAMPING = 0.8
CX, CY, NZ = 16, 64, 128
CR = 128
CAP = 40
BLOCK = CAP + 1
TRIO = 3 * BLOCK
W = 3
TOP = 8
EX, EY = CX + 2 * W, CY + 2 * TOP
F32, BF16, I32 = jnp.float32, jnp.bfloat16, jnp.int32

VMEM = pl.BlockSpec(memory_space=pltpu.VMEM)
SMEM = pl.BlockSpec(memory_space=pltpu.SMEM)


def iota(shape, dim):
    return lax.broadcasted_iota(I32, shape, dim)


def call(kernel, outs, args, in_specs=None, scratch=(), mib=16, aliases=None, out_specs=None):
    return pl.pallas_call(
        kernel,
        out_shape=[jax.ShapeDtypeStruct(s, d) for s, d in outs],
        in_specs=in_specs or [VMEM] * len(args),
        out_specs=out_specs or [VMEM] * len(outs),
        scratch_shapes=list(scratch),
        input_output_aliases=aliases or {},
        compiler_params=pltpu.CompilerParams(vmem_limit_bytes=mib << 20),
    )(*args)


def slot_kernel(owners, own_ref, row_ref, slot_ref, back_ref, buf_ref):
    shift = lax.rem(lax.axis_index("bulk"), 3) * BLOCK
    before = (iota((128, 128), 0) < iota((128, 128), 1)).astype(BF16)
    owner_of = iota((owners, 128), 0)
    lane_of = iota((128, 128), 0)
    seen = jnp.zeros((owners, 1), F32)
    numbers = jnp.zeros((owners, 128), F32)
    for b in range(own_ref.shape[0]):
        own = own_ref[b : b + 1, :]
        mine = owner_of == own
        mine_f = mine.astype(F32)
        count = jnp.dot(mine_f.astype(BF16), before, preferred_element_type=F32) + seen
        rank = jnp.sum(jnp.where(mine, count, 0.0), axis=0, keepdims=True).astype(I32)
        seen = seen + jnp.sum(mine_f, axis=1, keepdims=True)
        slot_ref[b : b + 1, :] = own * BLOCK + rank
        back_ref[b : b + 1, :] = own * CAP + rank
        named = jnp.where(lane_of == rank + shift, (row_ref[b : b + 1, :] + 1).astype(F32), 0.0)
        numbers = numbers + lax.dot_general(
            mine_f.astype(BF16), named.astype(BF16), (((1,), (1,)), ((), ())), preferred_element_type=F32
        )
    buf_ref[...] = jnp.zeros_like(buf_ref)
    for o in range(owners):
        buf_ref[o * BLOCK + CAP : o * BLOCK + BLOCK, :] = numbers[o : o + 1, :]


def edges():
    b, s = lax.axis_index("bulk"), lax.axis_index("slab")
    return b > 0, b < lax.axis_size("bulk") - 1, s > 0, s < lax.axis_size("slab") - 1


def zero_index():
    return jnp.minimum(lax.axis_index("bulk"), 0)


def keep(ok, values):
    return values if ok is None else jnp.where(ok, values, 0.0)


def plane_ok(e, xl, xh):
    return xl if e < W else (None if e < W + CX else xh)


def is_odd():
    return lax.rem(lax.axis_index("bulk"), 2) == 1


def send_kernel(p_ref, k_ref, r_ref, to_o, to_e, sems):
    odd = is_odd()
    copies = []
    at = 0
    for ref, n in ((p_ref, W), (k_ref, W), (r_ref, W - 1)):
        for dst, high in ((to_o, odd), (to_e, jnp.logical_not(odd))):
            src = ref.at[pl.ds(jnp.where(high, CX - n, 0), n)]
            copies.append(pltpu.make_async_copy(src, dst.at[pl.ds(at, n)], sems.at[len(copies)]))
        at += n
    for copy in copies:
        copy.start()
    for copy in copies:
        copy.wait()


def halo_plane(refs, a, e, rows):
    own, from_o, from_e, odd = refs[a], refs[3], refs[4], refs[5]
    if W <= e < W + CX:
        return own[e - W, rows, :]
    low = e < W
    i = W * a + (e - (1 if a == 2 else 0) if low else e - W - CX)
    of_o, of_e = from_o[i, rows, :], from_e[i, rows, :]
    return jnp.where(odd, of_e, of_o) if low else jnp.where(odd, of_o, of_e)


def side_kernel(p_ref, k_ref, r_ref, from_o, from_e, done, to_high, to_low):
    del done
    refs = (p_ref, k_ref, r_ref, from_o, from_e, is_odd())
    for e in range(1, EX - 1):
        at = 0
        for a, n in ((0, W), (1, W), (2, W - 1)):
            to_high[e - 1, at : at + n, :] = halo_plane(refs, a, e, slice(CY - n, CY))
            to_low[e - 1, at : at + n, :] = halo_plane(refs, a, e, slice(0, n))
            at += n


def prepare_rows(x, k_ref, wx, wy, wz, q, start, n, wy_start, ok, z):
    rows = pl.ds(start, n)
    k = k_ref[x, rows, :]
    low, high = k_ref[x, pl.ds(start - 1, n), :], k_ref[x, pl.ds(start + 1, n), :]
    wxl = k + k_ref[x - 1, rows, :]
    ks = jnp.where(z == 0, 0.0, pltpu.roll(k, 1, 1))
    kn = jnp.where(z == NZ - 1, 0.0, pltpu.roll(k, NZ - 1, 1))
    wzl = k + ks
    diagonal = (wxl + (k + k_ref[x + 1, rows, :])) + ((k + low) + (k + high)) + (wzl + (k + kn))
    ok = ok & (diagonal > 0.0)
    q[x, rows, :] = jnp.where(ok, DAMPING / jnp.where(ok, diagonal, 1.0), 0.0)
    wx[x, rows, :] = wxl
    wz[x, rows, :] = jnp.where(z == 0, 0.0, wzl)
    if wy_start is None:
        wy[x, rows, :] = k + low
    else:
        wy[x, pl.ds(wy_start, n), :] = k_ref[x, pl.ds(wy_start, n), :] + k_ref[x, pl.ds(wy_start - 1, n), :]


def neighbours(x, v_ref, wx, wy, wz, start, n, off):
    rows, below, above = pl.ds(start, n), pl.ds(off + (start - 1), n), pl.ds(off + (start + 1), n)
    v = v_ref[x, rows, :]
    wzl = wz[x, rows, :]
    total = wx[x, rows, :] * v_ref[x - 1, rows, :] + wx[x + 1, rows, :] * v_ref[x + 1, rows, :]
    total = total + (wy[x, rows, :] * v_ref[x, below, :] + wy[x, above, :] * v_ref[x, above, :])
    return v, total + (wzl * pltpu.roll(v, 1, 1) + pltpu.roll(wzl * v, NZ - 1, 1))


def sweep_rows(x, old, r2, wx, wy, wz, q, start, n, off):
    v, total = neighbours(x, old, wx, wy, wz, start, n, off)
    rows = pl.ds(start, n)
    return (1.0 - DAMPING) * v + q[x, rows, :] * (r2[x, rows, :] + total)


def residual_rows(x, old, r2, wx, wy, wz, q, start, n, off):
    v, total = neighbours(x, old, wx, wy, wz, start, n, off)
    rows = pl.ds(start, n)
    damped = q[x, rows, :]
    diagonal = DAMPING / jnp.where(damped == 0.0, 1.0, damped)
    return 0.5 * ((r2[x, rows, :] + total) - diagonal * v)


def fill(refs, fields, some, xl, xh):
    for a, dst in enumerate(fields):
        for e in some:
            if a == 2 and e in (0, EX - 1):
                continue
            values = keep(plane_ok(e, xl, xh), halo_plane(refs, a, e, slice(0, CY)))
            dst[e, TOP : TOP + CY, :] = values * 2.0 if a == 2 else values


def inner_steps(ranges, slot, buf, kx, rx, va, vb, vc, wx, wy, wz, q, res, xl, xh):
    off = zero_index()
    z = iota((CY, NZ), 1)
    own = pl.ds(TOP, CY)
    field = (rx, wx, wy, wz, q, TOP, CY, off)

    for lo, hi in ranges[0]:
        for x in range(lo, hi):
            ok = plane_ok(x, xl, xh)
            prepare_rows(x, kx, wx, wy, wz, q, TOP, CY, None, True if ok is None else ok, z)
        wx[hi, own, :] = kx[hi, own, :] + kx[hi - 1, own, :]
    for lo, hi in ranges[0]:
        for x in range(lo, hi):
            vb[x, own, :] = sweep_rows(x, va, *field)
    for lo, hi in ranges[1]:
        for x in range(lo, hi):
            vc[x, own, :] = sweep_rows(x, vb, *field)
    for lo, hi in ranges[2]:
        for x in range(lo, hi):
            at = (x - W) * CY
            res[at : at + CY, :] = residual_rows(x, vc, *field)
            for r in range(at + TOP, at + CY - TOP):
                buf[pl.ds(slot[r], 1), :] = res[r : r + 1, :]


def core_kernel(slot, p_ref, k_ref, r_ref, buf_in, buf, kx, rx, va, vb, vc, wx, wy, wz, q, res, done):
    del buf_in
    fill((p_ref, k_ref, r_ref, None, None, None), (va, kx, rx), range(W, W + CX), None, None)
    a, b = W + 1, W + CX - 1
    ranges = (((a, b),), ((a + 1, b - 1),), ((a + 2, b - 2),))
    inner_steps(ranges, slot, buf, kx, rx, va, vb, vc, wx, wy, wz, q, res, True, True)
    done[...] = jnp.zeros_like(done)


def mid_kernel(slot, from_o, from_e, *refs):
    buf, kx, rx, va, vb, vc, wx, wy, wz, q, res = refs[11:]
    xl, xh, _, _ = edges()
    halo = [*range(W), *range(W + CX, EX)]
    fill((None, None, None, from_o, from_e, is_odd()), (va, kx, rx), halo, xl, xh)
    a, b = W + 1, W + CX - 1
    ranges = tuple(((1 + i, a + i), (b - i, EX - 1 - i)) for i in range(3))
    inner_steps(ranges, slot, buf, kx, rx, va, vb, vc, wx, wy, wz, q, res, xl, xh)


def rim_kernel(
    slot_ref, sl, sh, kx_in, rx_in, va_in, vb_in, vc_in, wx_in, wy_in, wz_in, q_in, res, buf_in,
    kx, rx, va, vb, vc, wx, wy, wz, q, buf, slot, sem,
):
    del kx_in, rx_in, va_in, vb_in, vc_in, wx_in, wy_in, wz_in, q_in, buf_in, res
    table = pltpu.make_async_copy(slot_ref, slot, sem)
    table.start()
    xl, xh, yl, yh = edges()
    off = zero_index()
    end = TOP + CY
    for e in range(1, EX - 1):
        ok = plane_ok(e, xl, xh)
        low_ok, high_ok = (yl, yh) if ok is None else (yl & ok, yh & ok)
        for i, (dst, n, scale) in enumerate(((va, W, 1.0), (kx, W, 1.0), (rx, W - 1, 2.0))):
            at = W * i
            dst[e, TOP - n : TOP, :] = jnp.where(low_ok, sl[e - 1, at : at + n, :], 0.0) * scale
            dst[e, end : end + n, :] = jnp.where(high_ok, sh[e - 1, at : at + n, :], 0.0) * scale
    for e in (0, EX - 1):
        kx[e, TOP - W : TOP, :] = jnp.zeros((W, NZ), F32)
        kx[e, end : end + W, :] = jnp.zeros((W, NZ), F32)
        va[e, TOP - W : TOP, :] = jnp.zeros((W, NZ), F32)
        va[e, end : end + W, :] = jnp.zeros((W, NZ), F32)
    z, y = iota((8, NZ), 1), iota((8, NZ), 0)
    low_rows = (y >= 2) | yl
    high_rows = (y < 6) | yh
    field = (rx, wx, wy, wz, q)
    for x in range(1, EX - 1):
        ok = plane_ok(x, xl, xh)
        ok = True if ok is None else ok
        prepare_rows(x, kx, wx, wy, wz, q, off + (TOP - 2), 8, None, low_rows & ok, z)
        prepare_rows(x, kx, wx, wy, wz, q, off + (end - 6), 8, off + (end - 5), high_rows & ok, z)
    for start in (TOP - 2, end - 6):
        rows = pl.ds(off + start, 8)
        wx[EX - 1, rows, :] = kx[EX - 1, rows, :] + kx[EX - 2, rows, :]
    for x in range(1, EX - 1):
        for start in (TOP - 2, end - 6):
            vb[x, pl.ds(off + start, 8), :] = sweep_rows(x, va, *field, off + start, 8, 0)
    for x in range(2, EX - 2):
        for start in (TOP - 1, end - 7):
            vc[x, pl.ds(off + start, 8), :] = sweep_rows(x, vb, *field, off + start, 8, 0)
    table.wait()
    for x in range(CX):
        for start in (TOP, end - 8):
            out = residual_rows(x + W, vc, *field, start, 8, off)
            for u in range(8):
                buf[pl.ds(slot[x * CY + start - TOP + u], 1), :] = out[u : u + 1]


def parts_of(x):
    a = x.astype(BF16)
    rest = x - a.astype(F32)
    b = rest.astype(BF16)
    return a, b, (rest - b.astype(F32)).astype(BF16)


def coarse_kernel(owners, data, leak_ref, link_ref, back, hot, hot_back, parts):
    rows = owners * BLOCK
    groups = -(-owners // 3)
    pairs = -(-groups // 2)
    number = (iota((CR, 128), 0) + 1).astype(F32)
    for g in range(groups):
        base = g * TRIO
        names = [data[base + t * BLOCK + CAP : base + (t + 1) * BLOCK, :] for t in range(min(3, owners - 3 * g))]
        name = name_back = names[0]
        for t, more in enumerate(names[1:], 1):
            name = name + more
            name_back = name_back + pltpu.roll(jnp.broadcast_to(more, (8, 128)), 128 - t, 1)[0:1]
        if base + 128 > rows:
            name = pltpu.roll(jnp.broadcast_to(name, (8, 128)), base - (rows - 128), 1)[0:1]
            base = rows - 128
        at = g % 2 * 128
        hot_back[g // 2, :, at : at + 128] = jnp.where(number == name_back, 1.0, 0.0).astype(BF16)
        hot[:, g * 128 : (g + 1) * 128] = jnp.where(number == name, 1.0, 0.0).astype(BF16)
        for i, part in enumerate(parts_of(data[base : base + 128, :])):
            parts[g * 128 : (g + 1) * 128, i * NZ : (i + 1) * NZ] = part
    if groups % 2:
        hot_back[pairs - 1, :, 128:] = jnp.zeros((CR, 128), BF16)
    total = jnp.dot(hot[...], parts[...], preferred_element_type=F32)
    total = total[:, 0:NZ] + (total[:, NZ : 2 * NZ] + total[:, 2 * NZ :])

    z = iota((CR, NZ), 1)
    link = link_ref[...]
    inner = jnp.where(z == NZ - 1, 0.0, link)
    below = pltpu.roll(inner, 1, 1)
    w = DAMPING / (leak_ref[...] + link + below)
    u = w * total
    for _ in range(2):
        u = (1.0 - DAMPING) * u + w * (total + inner * pltpu.roll(u, NZ - 1, 1) + pltpu.roll(inner * u, 1, 1))
    pieces = jnp.concatenate(parts_of(u), axis=1)
    for p in range(pairs):
        out = lax.dot_general(hot_back[p], pieces, (((0,), (0,)), ((), ())), preferred_element_type=F32)
        out = out[:, 0:NZ] + (out[:, NZ : 2 * NZ] + out[:, 2 * NZ :])
        for g in (2 * p, 2 * p + 1):
            if g < groups:
                n = CAP * min(3, owners - 3 * g)
                at = g % 2 * 128
                back[3 * CAP * g : 3 * CAP * g + n, :] = out[at : at + n]


EDGE = (0, 1, CX - 2, CX - 1)


def edge_kernel(slot, back, vc, to_o, to_e):
    def fill_planes(low, high):
        for i, x in enumerate(EDGE):
            dst = low if i < 2 else high
            for y in range(CY):
                dst[i % 2, y : y + 1, :] = back[pl.ds(slot[x * CY + y], 1), :] + vc[x + W, TOP + y : TOP + y + 1, :]

    @pl.when(is_odd())
    def _():
        fill_planes(to_e, to_o)

    @pl.when(jnp.logical_not(is_odd()))
    def _():
        fill_planes(to_o, to_e)


def body_kernel(slot, back, vc, to_o, to_e, vd):
    odd = is_odd()
    for i, x in enumerate(EDGE):
        of_o, of_e = to_o[i % 2], to_e[i % 2]
        vd[x + W, TOP : TOP + CY, :] = jnp.where(odd, of_e, of_o) if i < 2 else jnp.where(odd, of_o, of_e)

    def plane(x, carry):
        for y in range(CY):
            row = back[pl.ds(slot[x * CY + y], 1), :] + vc[x + W, TOP + y : TOP + y + 1, :]
            vd[x + W, TOP + y : TOP + y + 1, :] = row
        return carry

    lax.fori_loop(2, CX - 2, plane, 0)


def last_side_kernel(vd, from_o, from_e, to_high, to_low):
    odd = is_odd()
    for dst, rows in ((to_high, slice(CY - 2, CY)), (to_low, slice(0, 2))):
        dst[0] = jnp.where(odd, from_e[1, rows, :], from_o[1, rows, :])
        dst[CX + 1] = jnp.where(odd, from_o[0, rows, :], from_e[0, rows, :])
        for x in range(CX):
            dst[x + 1] = vd[x + W, TOP + rows.start : TOP + rows.stop, :]


def last_inner_kernel(vd_in, from_o, from_e, rx, wx, wy, wz, q, vd, ve, out):
    del vd_in
    xl, xh, _, _ = edges()
    off = zero_index()
    own = pl.ds(TOP, CY)
    odd = is_odd()
    for e in (1, 2):
        of_o, of_e = from_o[e - 1], from_e[e - 1]
        vd[e, own, :] = jnp.where(xl, jnp.where(odd, of_e, of_o), 0.0)
        vd[e + CX + 2, own, :] = jnp.where(xh, jnp.where(odd, of_o, of_e), 0.0)

    field = (rx, wx, wy, wz, q, TOP, CY, off)

    for x in range(2, EX - 2):
        ve[x, own, :] = sweep_rows(x, vd, *field)
    for x in range(CX):
        out[x] = sweep_rows(x + W, ve, *field)


def last_rim_kernel(sl, sh, vd_in, ve_in, inner, rx, wx, wy, wz, q, vd, ve, out):
    del vd_in, ve_in
    xl, xh, yl, yh = edges()
    off = zero_index()
    end = TOP + CY
    for e in range(1, EX - 1):
        if 2 <= e < EX - 2:
            ok = plane_ok(e, xl, xh)
            low_ok, high_ok = (yl, yh) if ok is None else (yl & ok, yh & ok)
            vd[e, TOP - 2 : TOP, :] = jnp.where(low_ok, sl[e - 2], 0.0)
            vd[e, end : end + 2, :] = jnp.where(high_ok, sh[e - 2], 0.0)
        else:
            vd[e, TOP - 2 : TOP, :] = jnp.zeros((2, NZ), F32)
            vd[e, end : end + 2, :] = jnp.zeros((2, NZ), F32)

    field = (rx, wx, wy, wz, q)
    for x in range(2, EX - 2):
        for start in (TOP - 1, end - 7):
            ve[x, pl.ds(off + start, 8), :] = sweep_rows(x, vd, *field, off + start, 8, 0)
    for x in range(CX):
        out[x, 8 : CY - 8, :] = inner[x, 8 : CY - 8, :]
        for start in (TOP, end - 8):
            out[x, start - TOP : start - TOP + 8, :] = sweep_rows(x + W, ve, *field, start, 8, off)


def ring(axis, step):
    n = lax.axis_size(axis)
    return [(i, (i + step) % n) for i in range(n)]


def swap_both(to_o, to_e):
    n, m = lax.axis_size("bulk"), lax.axis_size("slab")
    got = []
    for first, values in ((1, to_o), (0, to_e)):
        pairs = [(i * m + s, (i + 1) * m + s) for i in range(first, n - 1, 2) for s in range(m)]
        if first:
            pairs += [(i * m + s, i * m + s + 1) for i in (0, n - 1) for s in range(0, m, 2)]
        got.append(lax.ppermute(values, ("bulk", "slab"), pairs + [(j, i) for i, j in pairs]))
    return got


def from_both(axis, to_high, to_low):
    low = lax.ppermute(to_high, axis, ring(axis, 1))
    high = lax.ppermute(to_low, axis, ring(axis, -1))
    return low, high


EXT = ((EX, EY, NZ), F32)


def cycle(pressure, rhs, kappa, owner, coarse_row, coarse_leak, coarse_link):
    owners = lax.axis_size("bulk")
    slots = owners * BLOCK
    sent = ((2 * W + W - 1, CY, NZ), F32)
    side = ((EX - 2, 8, NZ), F32)
    to_o, to_e = call(
        send_kernel,
        [sent, sent],
        [pltpu.with_memory_space_constraint(f, pltpu.MemorySpace.HBM) for f in (pressure, kappa, rhs)],
        in_specs=[pl.BlockSpec(memory_space=pltpu.MemorySpace.HBM)] * 3,
        scratch=[pltpu.SemaphoreType.DMA((6,))],
        mib=2,
    )
    from_o, from_e = swap_both(to_o, to_e)
    slot, slot_back, buf = call(
        lambda *refs: slot_kernel(owners, *refs),
        [((8, 128), I32), ((8, 128), I32), ((slots, NZ), F32)],
        (owner.reshape(8, 128), coarse_row.reshape(8, 128)),
    )
    table, table_back = slot.reshape(CX * CY), slot_back.reshape(CX * CY)
    work = [((slots, NZ), F32)] + [EXT] * 9 + [((CX * CY, NZ), F32)]
    *core, done = call(
        core_kernel,
        work + [((8, NZ), F32)],
        (table, pressure, kappa, rhs, buf),
        in_specs=[SMEM] + [VMEM] * 4,
        aliases={4: 0},
        mib=20,
    )
    to_high, to_low = call(side_kernel, [side, side], (pressure, kappa, rhs, from_o, from_e, done))
    sl, sh = from_both("slab", to_high, to_low)
    buf, *ext, res = call(
        mid_kernel,
        work,
        (table, from_o, from_e, *core),
        in_specs=[SMEM] + [VMEM] * 13,
        aliases={3 + i: i for i in range(11)},
        mib=20,
    )
    *ext, buf = call(
        rim_kernel,
        [EXT] * 9 + [((slots, NZ), F32)],
        (table, sl, sh, *ext, res, buf),
        aliases={**{3 + i: i for i in range(9)}, 13: 9},
        scratch=[pltpu.SMEM((CX * CY,), I32), pltpu.SemaphoreType.DMA],
        mib=20,
    )
    _, rx, _, _, vc, wx, wy, wz, q = ext
    got = lax.all_to_all(buf.reshape(owners, BLOCK, 1, NZ), "bulk", 0, 0)
    (back,) = call(
        lambda *refs: coarse_kernel(owners, *refs),
        [((owners * CAP, NZ), F32)],
        (got.reshape(slots, NZ), coarse_leak[0], coarse_link[0]),
        scratch=[
            pltpu.VMEM((CR, -(-owners // 3) * 128), BF16),
            pltpu.VMEM((-(-owners // 6), CR, 256), BF16),
            pltpu.VMEM((-(-owners // 3) * 128, 3 * NZ), BF16),
        ],
    )
    back = lax.all_to_all(back.reshape(owners, CAP, 1, NZ), "bulk", 0, 0).reshape(owners * CAP, NZ)
    to_o, to_e = call(
        edge_kernel, [((2, CY, NZ), F32)] * 2, (table_back, back, vc), in_specs=[SMEM, VMEM, VMEM]
    )
    from_o, from_e = swap_both(to_o, to_e)
    (vd,) = call(body_kernel, [EXT], (table_back, back, vc, to_o, to_e), in_specs=[SMEM] + [VMEM] * 4)

    last_side = ((CX + 2, 2, NZ), F32)
    to_high, to_low = call(last_side_kernel, [last_side, last_side], (vd, from_o, from_e))
    sl, sh = from_both("slab", to_high, to_low)
    vd, ve, inner = call(
        last_inner_kernel,
        [EXT, EXT, ((CX, CY, NZ), F32)],
        (vd, from_o, from_e, rx, wx, wy, wz, q),
        aliases={0: 0},
        mib=20,
    )
    _, _, out = call(
        last_rim_kernel,
        [EXT, EXT, ((CX, CY, NZ), F32)],
        (sl, sh, vd, ve, inner, rx, wx, wy, wz, q),
        aliases={2: 0, 3: 1},
        mib=20,
    )
    return out


def solution(mesh):
    return jax.shard_map(
        cycle,
        mesh=mesh,
        in_specs=(
            P("bulk", "slab", None),
            P("bulk", "slab", None),
            P("bulk", "slab", None),
            P("slab", "bulk", None, None),
            P("slab", "bulk", None),
            P("slab", "bulk", None),
            P("slab", "bulk", None),
        ),
        out_specs=P("bulk", "slab", None),
        check_vma=False,
    )
```
